128 devices in a mesh: scen: 4 (over y_lo, core), space: 32 (over x, z, y_hi).
Axes of the slice: x: 4, y: 4 (y_hi: 2, y_lo: 2; y = y_hi * 2 + y_lo), z: 4, core: 2. Of those that a mesh axis runs over, the one named last changes fastest.
Arguments:
- states: bfloat16 [3, 16, 3, 256, 32, 256], P(None, 'scen', None, 'space'), may hold values from 0.049804688 to 2
- terminal_adjoint: bfloat16 [16, 3, 256, 32, 256], P('scen', None, 'space'), may hold values from -6 to 6
- log_conductivity: float32 [256, 32, 256], P('space'), may hold values from -1 to 1
- log_rate: float32 [256, 32, 256], P('space'), may hold values from -1 to 1
- well_cell: int32 [16, 8], P('scen'), may hold values from 0 to 2097151
- sample_step: int32 [16, 8], P('scen'), may hold values from 1 to 2
- well_misfit: float32 [16, 8, 3], P('scen'), may hold values from -80 to 80
Outputs:
- update: float32 [2, 256, 32, 256], P(None, 'space', 'scen')
The draws below stay inside these ranges and needn't reach their ends.
Inputs may be any that keep to these rules, and one draw needn't show every extreme that they name: `well_cell`: a flat cell index x * 32 * 256 + z * 256 + y; wells may share a cell. `sample_step`: the reverse step at which the well's misfit enters the adjoint.
All inputs are finite; a program needn't handle non-finite values.
Results may differ from the reference program's by a relative error of at most 0.0003.
Values may be sent and summed in bfloat16 or wider, within the bound.
A program may use at most 128 MiB of HBM per device.

```python
import math
import jax
import jax.numpy as jnp
from jax import lax

NZ = 32
NY = 256
SPECIES = 3
STEPS = 3
WELLS = 8
SCEN = 16
NX = 256


def with_ends(values, rng, low, largest):
    place = [jax.random.randint(jax.random.fold_in(rng, axis), (), 0, length) for axis, length in enumerate(values.shape)]
    main_axis = values.shape.index(max(values.shape))
    next_to = place[:main_axis] + [(place[main_axis] + 1) % values.shape[main_axis]] + place[main_axis + 1:]
    return values.at[tuple(place)].set(low).at[tuple(next_to)].set(largest)


def block_scale(own_key, shape, split, low, largest):
    gain = 1.0
    for axis_at, parts in split:
        draws = jax.random.uniform(jax.random.fold_in(jax.random.fold_in(own_key, 6), axis_at), (parts,), jnp.float32, low / len(split), largest / len(split))
        gain = gain * jnp.repeat(jnp.exp(draws), shape[axis_at] // parts).reshape((-1,) + (1,) * (len(shape) - 1 - axis_at))
    return gain


def noise(rng, extent, deviation, most, pieces=(), kind=jnp.bfloat16):
    drawn = deviation * jax.random.normal(rng, extent, jnp.float32)
    if pieces:
        drawn = drawn * block_scale(rng, extent, pieces, -0.22, 0.18)
    return jnp.clip(drawn, -most, most).astype(kind)


def setup_inputs(seed: int = 0) -> dict:
    keys = jax.random.split(jax.random.key(seed), 8)
    states = jnp.clip(jnp.exp(math.log(2.0) - 3.6927934 * jax.random.uniform(keys[0], (STEPS, SCEN, SPECIES, NX, NZ, NY), jnp.float32) ** block_scale(keys[0], (STEPS, SCEN, SPECIES, NX, NZ, NY), ((1, 4), (3, 32)), -0.2, 0.2)), 0.049804688, 2.0).astype(jnp.bfloat16)
    terminal_adjoint = noise(keys[1], (SCEN, SPECIES, NX, NZ, NY), 1.0, 6.0, ((0, 4), (2, 32)))
    log_conductivity = jnp.clip(jax.random.uniform(keys[2], (NX, NZ, NY), jnp.float32, -1.0, 1.0) * block_scale(keys[2], (NX, NZ, NY), ((0, 32),), -0.4, 0.0), -1.0, 1.0)
    log_rate = jnp.clip(jax.random.uniform(keys[3], (NX, NZ, NY), jnp.float32, -1.0, 1.0) * block_scale(keys[3], (NX, NZ, NY), ((0, 32),), -0.4, 0.0), -1.0, 1.0)
    well_cell = with_ends(jax.random.randint(keys[4], (SCEN, WELLS), 0, NX * NZ * NY), jax.random.fold_in(keys[4], 1), 0, (NX * NZ * NY) - 1).astype(jnp.int32)
    sample_step = with_ends(jax.random.randint(keys[5], (SCEN, WELLS), 1, STEPS), jax.random.fold_in(keys[5], 1), 1, STEPS - 1).astype(jnp.int32)
    well_misfit = noise(keys[6], (SCEN, WELLS, SPECIES), 16.0, 80.0, ((0, 4),), jnp.float32)
    return dict(states=states, terminal_adjoint=terminal_adjoint, log_conductivity=log_conductivity, log_rate=log_rate, well_cell=well_cell, sample_step=sample_step, well_misfit=well_misfit)


time_step = 0.05
diffusion = (1.0, 0.8, 0.1)
donor_half = 0.5
acceptor_half = 0.3
acceptor_yield = 0.5
biomass_yield = 0.4
lengths = (40.0, 24.0)
offsets = ((1, 0, 0), (-1, 0, 0), (0, 1, 0), (0, -1, 0), (0, 0, 1), (0, 0, -1))

def views(padded, grid_shape):
    cells_x, cells_z, cells_y = grid_shape
    result = []
    for offset in offsets:
        step_x, step_z, step_y = offset
        result.append(padded[..., 1 + step_x:1 + step_x + cells_x, 1 + step_z:1 + step_z + cells_z, 1 + step_y:1 + step_y + cells_y])
    return result

def center_of(padded, grid_shape):
    cells_x, cells_z, cells_y = grid_shape
    return padded[..., 1:1 + cells_x, 1:1 + cells_z, 1:1 + cells_y]

def face_weights(cond_padded, grid_shape):
    middle = center_of(cond_padded, grid_shape)
    return [jnp.sqrt(middle * beside) for beside in views(cond_padded, grid_shape)]

def reverse_step(adjoint_pad, concen_pad, weights, uptake_rate, grid_shape, advance):
    adjoint = center_of(adjoint_pad, grid_shape)
    concen = center_of(concen_pad, grid_shape)
    diffusive = jnp.array(diffusion, jnp.float32).reshape(3, 1, 1, 1)
    cross_term = jnp.zeros_like(adjoint)
    spread = jnp.zeros_like(adjoint)
    for weight, adjoint_side, concen_side in zip(weights, views(adjoint_pad, grid_shape), views(concen_pad, grid_shape)):
        adjoint_diff = adjoint_side - adjoint
        cross_term = cross_term + weight * (concen_side - concen) * adjoint_diff
        spread = spread + weight * adjoint_diff
    grad_cond = -0.5 * time_step * lax.optimization_barrier(jnp.sum(diffusive * cross_term, axis=-4))
    donor_conc = concen[..., 0, :, :, :]
    accept_conc = concen[..., 1, :, :, :]
    biomass = concen[..., 2, :, :, :]
    donor_mono = donor_conc / (donor_half + donor_conc)
    accept_mono = accept_conc / (acceptor_half + accept_conc)
    reaction = uptake_rate * donor_mono * accept_mono * biomass
    stoich_sum = -adjoint[..., 0, :, :, :] - acceptor_yield * adjoint[..., 1, :, :, :] + biomass_yield * adjoint[..., 2, :, :, :]
    grad_rate = time_step * stoich_sum * reaction
    if not advance:
        return (None, grad_cond, grad_rate)
    rate_slopes = jnp.stack([uptake_rate * donor_half / (donor_half + donor_conc) ** 2 * accept_mono * biomass, uptake_rate * donor_mono * acceptor_half / (acceptor_half + accept_conc) ** 2 * biomass, uptake_rate * donor_mono * accept_mono], axis=-4)
    new_adjoint = adjoint + time_step * diffusive * spread + time_step * jnp.expand_dims(stoich_sum, -4) * rate_slopes
    return (new_adjoint, grad_cond, grad_rate)

def prior_spectrum(freq_x, freq_z, freq_y, count_x, count_z, count_y):
    wave_x = jnp.minimum(freq_x, count_x - freq_x).astype(jnp.float32) * (2.0 * math.pi / count_x)
    wave_z = jnp.minimum(freq_z, count_z - freq_z).astype(jnp.float32) * (2.0 * math.pi / count_z)
    wave_y = jnp.minimum(freq_y, count_y - freq_y).astype(jnp.float32) * (2.0 * math.pi / count_y)
    square = wave_x[:, None, None] ** 2 + wave_z[None, :, None] ** 2 + wave_y[None, None, :] ** 2
    fields = []
    for length in lengths:
        fields.append(length / jnp.sqrt(1.0 + length ** 2 * square))
    return jnp.stack(fields)

def reference(states, terminal_adjoint, log_conductivity, log_rate, well_cell, sample_step, well_misfit):
    grid_shape = (NX, NZ, NY)
    conductivity = jnp.exp(log_conductivity)
    uptake_rate = jnp.exp(log_rate)
    weights = face_weights(jnp.pad(conductivity, 1), grid_shape)
    pad_width = ((0, 0), (1, 1), (1, 1), (1, 1))

    def scenario(carry, index):
        total_cond, total_rate = carry
        adjoint = lax.dynamic_index_in_dim(terminal_adjoint, index, 0, False).astype(jnp.float32)
        cells = lax.dynamic_index_in_dim(well_cell, index, 0, False)
        sampled = lax.dynamic_index_in_dim(sample_step, index, 0, False)
        misfit = lax.dynamic_index_in_dim(well_misfit, index, 0, False)
        for step_index in range(STEPS - 1, -1, -1):
            concen = lax.dynamic_index_in_dim(states[step_index], index, 0, False).astype(jnp.float32)
            new_adjoint, grad_cond, grad_rate = reverse_step(jnp.pad(adjoint, pad_width), jnp.pad(concen, pad_width), weights, uptake_rate, grid_shape, step_index > 0)
            total_cond = total_cond + grad_cond
            total_rate = total_rate + grad_rate
            if step_index > 0:
                chosen = jnp.where(sampled == step_index, 1.0, 0.0).astype(jnp.float32)
                values = (misfit * chosen[:, None]).T
                flat = new_adjoint.reshape(SPECIES, -1).at[:, cells].add(values)
                adjoint = flat.reshape(new_adjoint.shape)
        return ((total_cond, total_rate), None)
    zeros = jnp.zeros(grid_shape, jnp.float32)
    totals, ignored = lax.scan(scenario, (zeros, zeros), jnp.arange(SCEN, dtype=jnp.int32))
    gradient = jnp.stack([totals[0], totals[1]])
    spectrum = prior_spectrum(jnp.arange(NX, dtype=jnp.int32), jnp.arange(NZ, dtype=jnp.int32), jnp.arange(NY, dtype=jnp.int32), NX, NZ, NY)
    half = spectrum[..., :NY // 2 + 1]
    spectral = jnp.fft.rfftn(gradient, axes=(1, 2, 3)) * half
    return jnp.fft.irfftn(spectral, s=grid_shape, axes=(1, 2, 3)).astype(jnp.float32)
```

```python
import functools
import math

import jax
import jax.numpy as jnp
import numpy as np
from jax import lax
from jax.experimental import pallas as pl
from jax.experimental.pallas import tpu as pltpu
from jax.sharding import PartitionSpec as P

time_step = 0.05
diffusion = (1.0, 0.8, 0.1)
donor_half = 0.5
acceptor_half = 0.3
acceptor_yield = 0.5
biomass_yield = 0.4
lengths = (40.0, 24.0)
f32 = jnp.float32
bf16 = jnp.bfloat16
MESH = pl.DeviceIdType.MESH

SL = 8
NZ = 32
NY = 256
NSC = 4
NW = 8
SP = 32
NX = SL * SP
LANES = 128


def cas(rows, cols, count):
    angle = 2.0 * np.pi * (np.outer(rows, cols) % count) / count
    return np.cos(angle) + np.sin(angle)


def two_parts(table):
    high = table.astype(np.float32).astype(bf16)
    low = (table - high.astype(np.float64)).astype(np.float32).astype(bf16)
    return np.stack([high, low])


def tables():
    count = np.arange(256)
    line = cas(count, count, 256)
    small = cas(np.arange(NZ), np.arange(NZ), NZ)
    ahead = np.zeros((NZ, SL, SL, NZ))
    back = np.zeros((4, SL, 8, NZ, SL))
    for x in range(SL):
        ahead[:, x, x, :] = small
        back[:, x, :, :, x] = small.reshape(4, 8, NZ)
    return np.stack(
        [two_parts(line), two_parts(ahead.reshape(256, 256)), two_parts(back.reshape(256, 256))]
    )


def split2(value):
    high = value.astype(bf16)
    low = (value - high.astype(f32)).astype(bf16)
    return high, low


def mm(a, b):
    return jnp.dot(a, b, preferred_element_type=f32)


def table_times(table, data):
    high, low = split2(data)
    return mm(table[0], high) + mm(table[0], low) + mm(table[1], high)


def times_table(data, table):
    high, low = split2(data)
    return mm(high, table[0]) + mm(low, table[0]) + mm(high, table[1])


def kernel(
    states,
    terminal,
    log_cond,
    log_rate,
    well_cell,
    sample_step,
    well_misfit,
    tabs_hbm,
    out,
    conc,
    adj3,
    adj2,
    adj1,
    cond,
    rate,
    weight_x,
    weight_z,
    weight_y,
    total_x,
    total_z,
    total_y,
    total_r,
    change,
    change_in,
    edge_in,
    hot,
    inject,
    tabs,
    spectrum,
    grad,
    part,
    part_in,
    half,
    half_in,
    column_out,
    column,
    back_out,
    back,
    block_out,
    block,
    local_sem,
    halo_send,
    halo_recv,
    sum_send,
    sum_recv,
    a2a_send,
    a2a_recv,
    b2a_send,
    b2a_recv,
    blk_send,
    blk_recv,
):
    scen = lax.axis_index("scen")
    space = lax.axis_index("space")
    left = lax.rem(space + SP - 1, SP)
    right = lax.rem(space + 1, SP)

    local = [
        pltpu.make_async_copy(terminal, adj3.at[:, :, 1 : 1 + SL], local_sem.at[0]),
        pltpu.make_async_copy(log_cond, cond.at[1 : 1 + SL], local_sem.at[1]),
        pltpu.make_async_copy(log_rate, rate, local_sem.at[2]),
        pltpu.make_async_copy(states.at[2], conc.at[2, :, :, 1 : 1 + SL], local_sem.at[3]),
        pltpu.make_async_copy(states.at[1], conc.at[1, :, :, 1 : 1 + SL], local_sem.at[4]),
        pltpu.make_async_copy(states.at[0], conc.at[0, :, :, 1 : 1 + SL], local_sem.at[5]),
        pltpu.make_async_copy(tabs_hbm, tabs, local_sem.at[6]),
    ]
    for copy in local:
        copy.start()

    barrier = pltpu.get_barrier_semaphore()

    def greet(i, carry):
        other = lax.rem(space + i, SP)
        pl.semaphore_signal(barrier, inc=1, device_id=(scen, other), device_id_type=MESH)
        return carry

    lax.fori_loop(1, SP, greet, 0)
    for i in range(1, 4):
        other = lax.rem(scen + i, 4)
        pl.semaphore_signal(barrier, inc=1, device_id=(other, space), device_id_type=MESH)
    pl.semaphore_wait(barrier, SP - 1 + 3)

    def to_side(i, source, target, side):
        return pltpu.make_async_remote_copy(
            src_ref=source,
            dst_ref=target,
            send_sem=halo_send.at[i],
            recv_sem=halo_recv.at[i],
            device_id=(scen, side),
            device_id_type=MESH,
        )

    halo = [
        to_side(0, log_cond.at[SL - 1], cond.at[0], right),
        to_side(1, log_cond.at[0], cond.at[SL + 1], left),
        to_side(2, terminal.at[:, :, SL - 1], adj3.at[:, :, 0], right),
        to_side(3, terminal.at[:, :, 0], adj3.at[:, :, SL + 1], left),
        to_side(4, states.at[0, :, :, SL - 1], conc.at[0, :, :, 0], right),
        to_side(5, states.at[0, :, :, 0], conc.at[0, :, :, SL + 1], left),
        to_side(6, change.at[1], change_in.at[0], right),
        to_side(7, change.at[0], change_in.at[1], left),
        to_side(8, total_x.at[SL], edge_in.at[0], right),
        to_side(9, total_x.at[0], edge_in.at[1], left),
    ]
    for i in range(6):
        halo[i].start()

    nothing = jnp.zeros((NZ, NY), f32)
    for s in range(NSC):
        for sp in range(3):
            for side in (0, SL + 1):
                conc[1, s, sp, side] = nothing.astype(bf16)
                conc[2, s, sp, side] = nothing.astype(bf16)
                adj1[s, sp, side] = nothing

    def clear(x, carry):
        total_x[x] = nothing
        total_z[x] = nothing
        total_y[x] = nothing
        total_r[x] = nothing
        return carry

    lax.fori_loop(0, SL, clear, 0)
    total_x[SL] = nothing

    lane = lax.broadcasted_iota(jnp.int32, (1, 32), 1)
    row_at = lax.broadcasted_iota(jnp.int32, (NZ, 32), 0)
    well_row = lax.broadcasted_iota(jnp.int32, (NW, NY), 0)
    well_col = lax.broadcasted_iota(jnp.int32, (NW, NY), 1)
    for s in range(NSC):
        row_of = jnp.full((1, 32), -1, jnp.int32)
        for w in range(NW):
            row = ((well_cell[s, w] - space * (SL * NZ * NY)) >> 8) + NZ
            row_of = jnp.where(lane % NW == w, row, row_of)
        row_of = jnp.where(lane < 3 * NW, row_of, -1)
        for x in range(SL + 2):
            hot[s, x] = jnp.where(row_at + x * NZ == row_of, 1.0, 0.0).astype(bf16)
        for n in (1, 2):
            for sp in range(3):
                value = jnp.zeros((NW, NY), f32)
                for w in range(NW):
                    amount = jnp.where(sample_step[s, w] == n, well_misfit[s, w, sp], 0.0)
                    here = (well_row == w) & (well_col == (well_cell[s, w] & 255))
                    value = jnp.where(here, amount, value)
                high = value.astype(bf16).astype(f32)
                rest = value - high
                middle = rest.astype(bf16).astype(f32)
                low = rest - middle
                inject[n, s, sp] = jnp.concatenate(
                    [high, middle, low, jnp.zeros((NW, NY), f32)], axis=0
                ).astype(bf16)

    local[1].wait()
    local[2].wait()
    z_index = lax.broadcasted_iota(jnp.int32, (NZ, NY), 0)
    y_index = lax.broadcasted_iota(jnp.int32, (NZ, NY), 1)

    def own_weights(x, carry):
        here = jnp.exp(cond[x])
        cond[x] = here
        rate[x - 1] = jnp.exp(rate[x - 1])
        above = jnp.sqrt(here * pltpu.roll(here, NZ - 1, 0))
        above = jnp.where(z_index == NZ - 1, 0.0, above)
        beside = jnp.sqrt(here * pltpu.roll(here, NY - 1, 1))
        beside = jnp.where(y_index == NY - 1, 0.0, beside)
        for sp in range(3):
            weight_z[sp, x - 1] = (time_step * diffusion[sp]) * above
            weight_y[sp, x - 1] = (time_step * diffusion[sp]) * beside
        return carry

    lax.fori_loop(1, SL + 1, own_weights, 0)

    def inner_weights(x, carry):
        between = jnp.sqrt(cond[x] * cond[x + 1])
        for sp in range(3):
            weight_x[sp, x] = (time_step * diffusion[sp]) * between
        return carry

    lax.fori_loop(1, SL, inner_weights, 0)

    def left_flux(adj, s, sp, x):
        here = adj[s, sp, x].astype(f32)
        return weight_x[sp, x - 1] * (here - adj[s, sp, x - 1].astype(f32))

    def layer(n, adj, new, s, x, side=None):
        own = x - 1
        conc_here = [conc[n, s, sp, x].astype(f32) for sp in range(3)]
        adj_here = [adj[s, sp, x].astype(f32) for sp in range(3)]
        sum_x = total_x[x]
        sum_z = total_z[own]
        sum_y = total_y[own]
        spread = []
        for sp in range(3):
            a, c = adj_here[sp], conc_here[sp]
            flux_x = weight_x[sp, x] * (adj[s, sp, x + 1].astype(f32) - a)
            flux_z = weight_z[sp, own] * (pltpu.roll(a, NZ - 1, 0) - a)
            flux_y = weight_y[sp, own] * (pltpu.roll(a, NY - 1, 1) - a)
            sum_x = sum_x + (conc[n, s, sp, x + 1].astype(f32) - c) * flux_x
            sum_z = sum_z + (pltpu.roll(c, NZ - 1, 0) - c) * flux_z
            sum_y = sum_y + (pltpu.roll(c, NY - 1, 1) - c) * flux_y
            if new is not None:
                spread.append(
                    (flux_x - left_flux(adj, s, sp, x))
                    + (flux_z - pltpu.roll(flux_z, 1, 0))
                    + (flux_y - pltpu.roll(flux_y, 1, 1))
                )
        total_x[x] = sum_x
        total_z[own] = sum_z
        total_y[own] = sum_y
        donor, acceptor, biomass = conc_here
        donor_inv = 1.0 / (donor_half + donor)
        accept_inv = 1.0 / (acceptor_half + acceptor)
        donor_mono = donor * donor_inv
        accept_mono = acceptor * accept_inv
        both = donor_mono * accept_mono
        stoich = -adj_here[0] - acceptor_yield * adj_here[1] + biomass_yield * adj_here[2]
        scaled = (time_step * stoich) * rate[own]
        growth = scaled * biomass
        total_r[own] = total_r[own] + growth * both
        if new is None:
            return
        spread[0] = spread[0] + (growth * accept_mono) * (donor_half * (donor_inv * donor_inv))
        spread[1] = spread[1] + (growth * donor_mono) * (acceptor_half * (accept_inv * accept_inv))
        spread[2] = spread[2] + scaled * both
        rows = hot[s, x]
        for sp in range(3):
            if side is not None:
                change[side, s, sp] = spread[sp].astype(bf16)
            new[s, sp, x] = adj_here[sp] + spread[sp] + mm(rows, inject[n, s, sp])

    def left_face(n, adj):
        def one(s, carry):
            sum_x = total_x[0]
            for sp in range(3):
                step_c = conc[n, s, sp, 1].astype(f32) - conc[n, s, sp, 0].astype(f32)
                sum_x = sum_x + step_c * left_flux(adj, s, sp, 1)
            total_x[0] = sum_x
            return carry

        lax.fori_loop(0, NSC, one, 0)

    def layers(n, adj, new, first, last):
        def one(i, carry):
            layer(n, adj, new, lax.rem(i, NSC), first + i // NSC)
            return carry

        lax.fori_loop(0, (last - first) * NSC, one, 0)

    def edges(n, adj, new, send):
        for side, x in ((0, 1), (1, SL)):

            def one(s, carry):
                layer(n, adj, new, s, x, side if send else None)
                return carry

            lax.fori_loop(0, NSC, one, 0)

    local[0].wait()
    local[3].wait()
    layers(2, adj3, adj2, 2, SL)
    for i in range(4):
        halo[i].wait_recv()
    no_left = space == 0
    no_right = space == SP - 1
    between = jnp.sqrt(jnp.exp(cond[0]) * cond[1])
    between = jnp.where(no_left, 0.0, between)
    for sp in range(3):
        weight_x[sp, 0] = (time_step * diffusion[sp]) * between
    between = jnp.sqrt(cond[SL] * jnp.exp(cond[SL + 1]))
    between = jnp.where(no_right, 0.0, between)
    for sp in range(3):
        weight_x[sp, SL] = (time_step * diffusion[sp]) * between
    edges(2, adj3, adj2, True)
    halo[6].start()
    halo[7].start()
    left_face(2, adj3)

    local[4].wait()
    layers(1, adj2, adj1, 2, SL)

    row = lax.broadcasted_iota(jnp.int32, (NX, LANES), 0)
    col = lax.broadcasted_iota(jnp.int32, (NX, LANES), 1)
    wave_x = jnp.minimum(row, NX - row).astype(f32) * (2.0 * math.pi / NX)
    freq_y = scen * 64 + col % 64
    wave_y = jnp.minimum(freq_y, NY - freq_y).astype(f32) * (2.0 * math.pi / NY)
    freq_z = jnp.full((1, LANES), space, jnp.int32)
    wave_z = jnp.minimum(freq_z, NZ - freq_z).astype(f32) * (2.0 * math.pi / NZ)
    field = (col // 64 + scen) % 2
    length = jnp.where(field == 0, lengths[0], lengths[1])
    square = wave_x * wave_x + wave_z * wave_z + wave_y * wave_y
    spectrum[...] = (length / jnp.sqrt(1.0 + (length * length) * square)) * (1.0 / (NX * NZ * NY))

    halo[6].wait_recv()
    halo[7].wait_recv()

    def halo_layers(s, carry):
        for side, x in ((0, 0), (1, SL + 1)):
            rows = hot[s, x]
            for sp in range(3):
                adj2[s, sp, x] = (
                    adj3[s, sp, x].astype(f32)
                    + change_in[side, s, sp].astype(f32)
                    + mm(rows, inject[2, s, sp])
                )
        return carry

    lax.fori_loop(0, NSC, halo_layers, 0)
    edges(1, adj2, adj1, False)
    left_face(1, adj2)

    local[5].wait()
    halo[4].wait_recv()
    halo[5].wait_recv()
    left_face(0, adj1)
    layers(0, adj1, None, SL, SL + 1)
    halo[8].start()
    halo[9].start()
    layers(0, adj1, None, 1, SL)

    def inner_grad(x):
        along_z = total_z[x]
        along_y = total_y[x]
        return (
            along_z + pltpu.roll(along_z, 1, 0) + along_y + pltpu.roll(along_y, 1, 1)
        )

    def gradients(x, carry):
        grad[0, x] = -0.5 * (inner_grad(x) + total_x[x] + total_x[x + 1])
        grad[1, x] = total_r[x]
        return carry

    lax.fori_loop(1, SL - 1, gradients, 0)
    halo[8].wait_recv()
    halo[9].wait_recv()
    grad[0, 0] = -0.5 * (inner_grad(0) + total_x[0] + edge_in[0] + total_x[1])
    grad[1, 0] = total_r[0]
    grad[0, SL - 1] = -0.5 * (inner_grad(SL - 1) + total_x[SL - 1] + total_x[SL] + edge_in[1])
    grad[1, SL - 1] = total_r[SL - 1]
    for copy in halo:
        copy.wait_send()

    local[6].wait()
    first = lax.broadcasted_iota(jnp.int32, (256, LANES), 1) < 64
    cond_y = times_table(grad[0].reshape(256, NY), tabs[0])
    rate_y = times_table(grad[1].reshape(256, NY), tabs[0])
    for chip in range(2):
        lanes = slice(chip * LANES, (chip + 1) * LANES)
        a = cond_y[:, lanes]
        b = pltpu.roll(rate_y[:, lanes], 64, 1)
        part[0, chip] = jnp.where(first, a, b)
        part[1, chip] = jnp.where(first, b, a)

    chip = scen // 2
    core = lax.rem(scen, 2)
    mate = (chip * 2 + 1 - core, space)
    far = ((1 - chip) * 2 + core, space)
    near_copies = []
    for i, which in enumerate((1 - chip, chip)):
        near_copies.append(
            pltpu.make_async_remote_copy(
                src_ref=part.at[1 - core, which],
                dst_ref=part_in.at[i],
                send_sem=sum_send.at[i],
                recv_sem=sum_recv.at[i],
                device_id=mate,
                device_id_type=MESH,
            )
        )
    for copy in near_copies:
        copy.start()
    near_copies[0].wait_recv()
    half[...] = part[core, 1 - chip] + part_in[0]
    far_copy = pltpu.make_async_remote_copy(
        src_ref=half,
        dst_ref=half_in,
        send_sem=sum_send.at[2],
        recv_sem=sum_recv.at[2],
        device_id=far,
        device_id_type=MESH,
    )
    far_copy.start()
    near_copies[1].wait_recv()
    mine = part[core, chip] + part_in[1]
    far_copy.wait_recv()
    mine = mine + half_in[...]

    column_out[...] = table_times(tabs[1], mine).reshape(SP, SL, LANES)

    def exchange(source, target, send, recv):
        def copy_of(i):
            other = lax.rem(space + i, SP)
            return pltpu.make_async_remote_copy(
                src_ref=source.at[other],
                dst_ref=target.at[space],
                send_sem=send.at[i],
                recv_sem=recv.at[i],
                device_id=(scen, other),
                device_id_type=MESH,
            )

        def begin(i, carry):
            copy_of(i).start()
            return carry

        def arrive(i, carry):
            copy_of(i).wait()
            return carry

        lax.fori_loop(1, SP, begin, 0)
        target[space] = source[space]
        lax.fori_loop(1, SP, arrive, 0)

    exchange(column_out, column, a2a_send, a2a_recv)
    spectral = table_times(tabs[0], column[...].reshape(NX, LANES)) * spectrum[...]
    back_out[...] = table_times(tabs[0], spectral).reshape(SP, SL, LANES)
    exchange(back_out, back, b2a_send, b2a_recv)

    block_out[...] = table_times(tabs[2], back[...].reshape(256, LANES)).reshape(4, 64, LANES)
    block_copies = []
    for i in range(1, 4):
        other = lax.rem(scen + i, 4)
        block_copies.append(
            pltpu.make_async_remote_copy(
                src_ref=block_out.at[other],
                dst_ref=block.at[scen],
                send_sem=blk_send.at[i],
                recv_sem=blk_recv.at[i],
                device_id=(other, space),
                device_id_type=MESH,
            )
        )
    for copy in block_copies:
        copy.start()
    block[scen] = block_out[scen]
    for copy in block_copies:
        copy.wait()
    for copy in near_copies:
        copy.wait_send()
    far_copy.wait_send()

    first = lax.broadcasted_iota(jnp.int32, (64, LANES), 1) < 64
    cond_f = [jnp.where(first, block[i], block[i + 1]) for i in (0, 2)]
    rate_f = [pltpu.roll(jnp.where(first, block[i + 1], block[i]), 64, 1) for i in (0, 2)]
    for field, halves in enumerate((cond_f, rate_f)):
        whole = jnp.concatenate(halves, axis=1)
        out[field] = times_table(whole, tabs[0]).reshape(SL, 8, NY)


def body(states, terminal, log_cond, log_rate, well_cell, sample_step, well_misfit):
    hbm = pl.BlockSpec(memory_space=pl.ANY)
    smem = pl.BlockSpec(memory_space=pltpu.SMEM)
    vmem = pl.BlockSpec(memory_space=pltpu.VMEM)
    dma = pltpu.SemaphoreType.DMA
    slab = (SL, NZ, NY)
    scratch = [
        pltpu.VMEM((3, NSC, 3, SL + 2, NZ, NY), bf16),
        pltpu.VMEM((NSC, 3, SL + 2, NZ, NY), bf16),
        pltpu.VMEM((NSC, 3, SL + 2, NZ, NY), f32),
        pltpu.VMEM((NSC, 3, SL + 2, NZ, NY), f32),
        pltpu.VMEM((SL + 2, NZ, NY), f32),
        pltpu.VMEM(slab, f32),
        pltpu.VMEM((3, SL + 1, NZ, NY), f32),
        pltpu.VMEM((3,) + slab, f32),
        pltpu.VMEM((3,) + slab, f32),
        pltpu.VMEM((SL + 1, NZ, NY), f32),
        pltpu.VMEM(slab, f32),
        pltpu.VMEM(slab, f32),
        pltpu.VMEM(slab, f32),
        pltpu.VMEM((2, NSC, 3, NZ, NY), bf16),
        pltpu.VMEM((2, NSC, 3, NZ, NY), bf16),
        pltpu.VMEM((2, NZ, NY), f32),
        pltpu.VMEM((NSC, SL + 2, NZ, 32), bf16),
        pltpu.VMEM((3, NSC, 3, 32, NY), bf16),
        pltpu.VMEM((3, 2, 256, 256), bf16),
        pltpu.VMEM((NX, LANES), f32),
        pltpu.VMEM((2,) + slab, f32),
        pltpu.VMEM((2, 2, 256, LANES), f32),
        pltpu.VMEM((2, 256, LANES), f32),
        pltpu.VMEM((256, LANES), f32),
        pltpu.VMEM((256, LANES), f32),
        pltpu.VMEM((SP, SL, LANES), f32),
        pltpu.VMEM((SP, SL, LANES), f32),
        pltpu.VMEM((SP, SL, LANES), f32),
        pltpu.VMEM((SP, SL, LANES), f32),
        pltpu.VMEM((4, 64, LANES), f32),
        pltpu.VMEM((4, 64, LANES), f32),
        dma((7,)),
        dma((10,)),
        dma((10,)),
        dma((3,)),
        dma((3,)),
        dma((SP,)),
        dma((SP,)),
        dma((SP,)),
        dma((SP,)),
        dma((4,)),
        dma((4,)),
    ]
    return pl.pallas_call(
        kernel,
        out_shape=jax.ShapeDtypeStruct((2, SL, 8, NY), f32),
        in_specs=[hbm, hbm, hbm, hbm, smem, smem, smem, hbm],
        out_specs=vmem,
        scratch_shapes=scratch,
        compiler_params=pltpu.CompilerParams(
            collective_id=0, has_side_effects=True, vmem_limit_bytes=60 * 1024 * 1024
        ),
    )(
        states,
        terminal,
        log_cond,
        log_rate,
        well_cell,
        sample_step,
        well_misfit,
        jnp.asarray(tables()),
    )


def solution(mesh):
    in_specs = (
        P(None, "scen", None, "space", None, None),
        P("scen", None, "space", None, None),
        P("space", None, None),
        P("space", None, None),
        P("scen", None),
        P("scen", None),
        P("scen", None, None),
    )
    out_specs = P(None, "space", "scen", None)
    return jax.shard_map(body, mesh=mesh, in_specs=in_specs, out_specs=out_specs, check_vma=False)
```

```python
import functools
import math

import jax
import jax.numpy as jnp
import numpy as np
from jax import lax
from jax.experimental import pallas as pl
from jax.experimental.pallas import tpu as pltpu
from jax.sharding import PartitionSpec as P

time_step = 0.05
diffusion = (1.0, 0.8, 0.1)
donor_half = 0.5
acceptor_half = 0.3
acceptor_yield = 0.5
biomass_yield = 0.4
lengths = (40.0, 24.0)
f32 = jnp.float32
bf16 = jnp.bfloat16
MESH = pl.DeviceIdType.MESH

SL = 8
NZ = 32
NY = 256
NSC = 4
NW = 8
SP = 32
NX = SL * SP
LANES = 128


def cas(rows, cols, count):
    angle = 2.0 * np.pi * (np.outer(rows, cols) % count) / count
    return np.cos(angle) + np.sin(angle)


def two_parts(table):
    high = table.astype(np.float32).astype(bf16)
    low = (table - high.astype(np.float64)).astype(np.float32).astype(bf16)
    return np.stack([high, low])


def tables():
    count = np.arange(256)
    line = cas(count, count, 256)
    small = cas(np.arange(NZ), np.arange(NZ), NZ)
    ahead = np.zeros((NZ, SL, SL, NZ))
    back = np.zeros((4, SL, 8, NZ, SL))
    for x in range(SL):
        ahead[:, x, x, :] = small
        back[:, x, :, :, x] = small.reshape(4, 8, NZ)
    corner = np.zeros((256, 256))
    corner[:NZ, :NZ] = small
    turned = [line, ahead.reshape(256, 256), back.reshape(256, 256), corner]
    return np.stack([two_parts(table) for table in turned])


def split2(value):
    high = value.astype(bf16)
    low = (value - high.astype(f32)).astype(bf16)
    return high, low


def mm(a, b):
    return jnp.dot(a, b, preferred_element_type=f32)


def table_times(table, data):
    high, low = split2(data)
    return mm(table[0], high) + mm(table[0], low) + mm(table[1], high)


def times_table(data, table):
    high, low = split2(data)
    return mm(high, table[0]) + mm(low, table[0]) + mm(high, table[1])


def kernel(
    states,
    terminal,
    log_cond,
    log_rate,
    well_cell,
    sample_step,
    misfit_hbm,
    tabs_hbm,
    out,
    conc,
    adj3,
    adj2,
    adj1,
    cond,
    rate,
    weight_x,
    weight_z,
    weight_y,
    total_x,
    total_z,
    total_y,
    total_r,
    change,
    change_in,
    misfit,
    hot,
    inject,
    tabs,
    spectrum,
    grad,
    part,
    part_in,
    rim,
    rim_in,
    column_out,
    column,
    back_out,
    back,
    block_out,
    block,
    local_sem,
    halo_send,
    halo_recv,
    sum_send,
    sum_recv,
    a2a_send,
    a2a_recv,
    b2a_send,
    b2a_recv,
    blk_send,
    blk_recv,
):
    scen = lax.axis_index("scen")
    space = lax.axis_index("space")
    chip = scen // 2
    core = lax.rem(scen, 2)
    left = lax.rem(space + SP - 1, SP)
    right = lax.rem(space + 1, SP)

    local = [
        pltpu.make_async_copy(terminal, adj3.at[:, :, 1 : 1 + SL], local_sem.at[0]),
        pltpu.make_async_copy(log_cond, cond.at[1 : 1 + SL], local_sem.at[1]),
        pltpu.make_async_copy(log_rate, rate, local_sem.at[2]),
        pltpu.make_async_copy(misfit_hbm, misfit, local_sem.at[3]),
        pltpu.make_async_copy(states.at[2], conc.at[2, :, :, 1 : 1 + SL], local_sem.at[4]),
        pltpu.make_async_copy(states.at[1], conc.at[1, :, :, 1 : 1 + SL], local_sem.at[5]),
        pltpu.make_async_copy(states.at[0], conc.at[0, :, :, 1 : 1 + SL], local_sem.at[6]),
        pltpu.make_async_copy(tabs_hbm, tabs, local_sem.at[7]),
    ]
    for copy in local:
        copy.start()

    barrier = pltpu.get_barrier_semaphore()

    def signal(to_scen, to_space):
        pl.semaphore_signal(
            barrier, inc=1, device_id=(to_scen, to_space), device_id_type=MESH
        )

    def greet(i, carry):
        other = lax.rem(space + i, SP)
        signal(scen, other)
        signal((1 - chip) * 2 + core, other)
        return carry

    signal((1 - chip) * 2 + core, space)
    signal(chip * 2 + 1 - core, space)
    signal((1 - chip) * 2 + 1 - core, space)
    lax.fori_loop(1, SP, greet, 0)
    pl.semaphore_wait(barrier, 2 * (SP - 1) + 3)

    def to_side(i, source, target, side):
        return pltpu.make_async_remote_copy(
            src_ref=source,
            dst_ref=target,
            send_sem=halo_send.at[i],
            recv_sem=halo_recv.at[i],
            device_id=(scen, side),
            device_id_type=MESH,
        )

    def cond_halo():
        return (
            to_side(0, log_cond.at[SL - 1], cond.at[0], right),
            to_side(1, log_cond.at[0], cond.at[SL + 1], left),
        )

    def adj_halo(s):
        return (
            to_side(2 + s, terminal.at[s, :, SL - 1], adj3.at[s, :, 0], right),
            to_side(6 + s, terminal.at[s, :, 0], adj3.at[s, :, SL + 1], left),
        )

    def change_halo(s):
        return (
            to_side(10 + s, change.at[1, s], change_in.at[0, s], right),
            to_side(14 + s, change.at[0, s], change_in.at[1, s], left),
        )

    def conc_halo(s):
        return (
            to_side(18 + s, states.at[0, s, :, SL - 1], conc.at[0, s, :, 0], right),
            to_side(22 + s, states.at[0, s, :, 0], conc.at[0, s, :, SL + 1], left),
        )

    for copy in cond_halo():
        copy.start()
    for s in range(NSC):
        for copy in adj_halo(s):
            copy.start()

    nothing = jnp.zeros((NZ, NY), f32)
    for s in range(NSC):
        for sp in range(3):
            for side in (0, SL + 1):
                conc[1, s, sp, side] = nothing.astype(bf16)
                conc[2, s, sp, side] = nothing.astype(bf16)
                adj1[s, sp, side] = nothing

    def clear(x, carry):
        total_x[x] = nothing
        total_z[x] = nothing
        total_y[x] = nothing
        total_r[x] = nothing
        return carry

    lax.fori_loop(0, SL, clear, 0)
    total_x[SL] = nothing

    local[1].wait()
    local[2].wait()
    z_index = lax.broadcasted_iota(jnp.int32, (NZ, NY), 0)
    y_index = lax.broadcasted_iota(jnp.int32, (NZ, NY), 1)

    def own_weights(x, carry):
        here = jnp.exp(cond[x])
        cond[x] = here
        rate[x - 1] = jnp.exp(rate[x - 1])
        above = jnp.sqrt(here * pltpu.roll(here, NZ - 1, 0))
        above = jnp.where(z_index == NZ - 1, 0.0, above)
        beside = jnp.sqrt(here * pltpu.roll(here, NY - 1, 1))
        beside = jnp.where(y_index == NY - 1, 0.0, beside)
        for sp in range(3):
            weight_z[sp, x - 1] = (time_step * diffusion[sp]) * above
            weight_y[sp, x - 1] = (time_step * diffusion[sp]) * beside
        return carry

    lax.fori_loop(1, SL + 1, own_weights, 0)

    def inner_weights(x, carry):
        between = jnp.sqrt(cond[x] * cond[x + 1])
        for sp in range(3):
            weight_x[sp, x] = (time_step * diffusion[sp]) * between
        return carry

    lax.fori_loop(1, SL, inner_weights, 0)

    local[3].wait()
    lane = lax.broadcasted_iota(jnp.int32, (1, 32), 1)
    row_at = lax.broadcasted_iota(jnp.int32, (NZ, 32), 0)
    well_row = lax.broadcasted_iota(jnp.int32, (NW, NY), 0)
    well_col = lax.broadcasted_iota(jnp.int32, (NW, NY), 1)

    def wells(s, carry):
        row_of = jnp.full((1, 32), -1, jnp.int32)
        col_of = jnp.zeros((NW, NY), jnp.int32)
        step_of = jnp.zeros((NW, NY), jnp.int32)
        for w in range(NW):
            cell = well_cell[s, w]
            row = ((cell - space * (SL * NZ * NY)) >> 8) + NZ
            row_of = jnp.where(lane % NW == w, row, row_of)
            col_of = jnp.where(well_row == w, cell & 255, col_of)
            step_of = jnp.where(well_row == w, sample_step[s, w], step_of)
        row_of = jnp.where(lane < 3 * NW, row_of, -1)
        for x in range(SL + 2):
            hot[s, x] = jnp.where(row_at + x * NZ == row_of, 1.0, 0.0).astype(bf16)
        here = well_col == col_of
        amount = misfit[s]
        for n in (1, 2):
            chosen = here & (step_of == n)
            for sp in range(3):
                value = jnp.where(chosen, amount[:, sp : sp + 1], 0.0)
                high = value.astype(bf16).astype(f32)
                rest = value - high
                middle = rest.astype(bf16).astype(f32)
                low = rest - middle
                inject[n, s, sp] = jnp.concatenate(
                    [high, middle, low, jnp.zeros((NW, NY), f32)], axis=0
                ).astype(bf16)
        return carry

    lax.fori_loop(0, NSC, wells, 0)

    def x_flux(adj, s, sp, x):
        before = adj[s, sp, x].astype(f32)
        return weight_x[sp, x] * (adj[s, sp, x + 1].astype(f32) - before)

    def layer(n, adj, new, s, x, side=None, face=True):
        own = x - 1
        conc_here = [conc[n, s, sp, x].astype(f32) for sp in range(3)]
        adj_here = [adj[s, sp, x].astype(f32) for sp in range(3)]
        sum_x = total_x[x]
        sum_z = total_z[own]
        sum_y = total_y[own]
        spread = []
        for sp in range(3):
            a, c = adj_here[sp], conc_here[sp]
            flux_z = weight_z[sp, own] * (pltpu.roll(a, NZ - 1, 0) - a)
            flux_y = weight_y[sp, own] * (pltpu.roll(a, NY - 1, 1) - a)
            sum_z = sum_z + (pltpu.roll(c, NZ - 1, 0) - c) * flux_z
            sum_y = sum_y + (pltpu.roll(c, NY - 1, 1) - c) * flux_y
            if face:
                flux_x = x_flux(adj, s, sp, x)
                sum_x = sum_x + (conc[n, s, sp, x + 1].astype(f32) - c) * flux_x
            if new is not None:
                spread.append(
                    (flux_x - x_flux(adj, s, sp, x - 1))
                    + (flux_z - pltpu.roll(flux_z, 1, 0))
                    + (flux_y - pltpu.roll(flux_y, 1, 1))
                )
        if face:
            total_x[x] = sum_x
        total_z[own] = sum_z
        total_y[own] = sum_y
        donor, acceptor, biomass = conc_here
        donor_inv = 1.0 / (donor_half + donor)
        accept_inv = 1.0 / (acceptor_half + acceptor)
        donor_mono = donor * donor_inv
        accept_mono = acceptor * accept_inv
        both = donor_mono * accept_mono
        stoich = -adj_here[0] - acceptor_yield * adj_here[1] + biomass_yield * adj_here[2]
        scaled = (time_step * stoich) * rate[own]
        growth = scaled * biomass
        total_r[own] = total_r[own] + growth * both
        if new is None:
            return
        spread[0] = spread[0] + (growth * accept_mono) * (donor_half * (donor_inv * donor_inv))
        spread[1] = spread[1] + (growth * donor_mono) * (acceptor_half * (accept_inv * accept_inv))
        spread[2] = spread[2] + scaled * both
        rows = hot[s, x]
        for sp in range(3):
            if side is not None:
                change[side, s, sp] = spread[sp].astype(bf16)
            new[s, sp, x] = adj_here[sp] + spread[sp] + mm(rows, inject[n, s, sp])

    def x_face(n, adj, s, x):
        total = total_x[x]
        for sp in range(3):
            step_c = conc[n, s, sp, x + 1].astype(f32) - conc[n, s, sp, x].astype(f32)
            total = total + step_c * x_flux(adj, s, sp, x)
        total_x[x] = total

    def layers(n, adj, new, s, first, last):
        def one(x, carry):
            layer(n, adj, new, s, x)
            return carry

        lax.fori_loop(first, last, one, 0)

    local[0].wait()
    local[4].wait()

    def inner_two(s, carry):
        layers(2, adj3, adj2, s, 2, SL)
        return carry

    lax.fori_loop(0, NSC, inner_two, 0)
    for copy in cond_halo():
        copy.wait_recv()
    for x, beyond, wall in ((0, 0, space == 0), (SL, SL + 1, space == SP - 1)):
        between = jnp.sqrt(jnp.exp(cond[beyond]) * cond[2 * x + 1 - beyond])
        between = jnp.where(wall, 0.0, between)
        for sp in range(3):
            weight_x[sp, x] = (time_step * diffusion[sp]) * between
    local[5].wait()

    def two_and_one(s, carry):
        for copy in adj_halo(s):
            copy.wait_recv()
        layer(2, adj3, adj2, s, 1, 0)
        layer(2, adj3, adj2, s, SL, 1)
        for copy in change_halo(s):
            copy.start()
        x_face(2, adj3, s, 0)
        layers(1, adj2, adj1, s, 2, SL)
        return carry

    lax.fori_loop(0, NSC, two_and_one, 0)
    for s in range(NSC):
        for copy in conc_halo(s):
            copy.start()

    row = lax.broadcasted_iota(jnp.int32, (NX, LANES), 0)
    col = lax.broadcasted_iota(jnp.int32, (NX, LANES), 1)
    wave_x = jnp.minimum(row, NX - row).astype(f32) * (2.0 * math.pi / NX)
    freq_y = scen * 64 + col % 64
    wave_y = jnp.minimum(freq_y, NY - freq_y).astype(f32) * (2.0 * math.pi / NY)
    freq_z = jnp.full((1, LANES), space, jnp.int32)
    wave_z = jnp.minimum(freq_z, NZ - freq_z).astype(f32) * (2.0 * math.pi / NZ)
    field = (col // 64 + scen) % 2
    length = jnp.where(field == 0, lengths[0], lengths[1])
    square = wave_x * wave_x + wave_z * wave_z + wave_y * wave_y
    spectrum[...] = (length / jnp.sqrt(1.0 + (length * length) * square)) * (1.0 / (NX * NZ * NY))
    local[6].wait()

    def one_and_none(s, carry):
        for copy in change_halo(s):
            copy.wait_recv()
        for side, x in ((0, 0), (1, SL + 1)):
            rows = hot[s, x]
            for sp in range(3):
                adj2[s, sp, x] = (
                    adj3[s, sp, x].astype(f32)
                    + change_in[side, s, sp].astype(f32)
                    + mm(rows, inject[2, s, sp])
                )
        layer(1, adj2, adj1, s, 1)
        layer(1, adj2, adj1, s, SL)
        x_face(1, adj2, s, 0)
        layers(0, adj1, None, s, 1, SL)
        layer(0, adj1, None, s, SL, face=False)
        return carry

    lax.fori_loop(0, NSC, one_and_none, 0)

    def gradients(x, carry):
        along_z = total_z[x]
        along_y = total_y[x]
        total = along_z + pltpu.roll(along_z, 1, 0) + along_y + pltpu.roll(along_y, 1, 1)
        before = jnp.where(x == 0, 0.0, total_x[x])
        after = jnp.where(x == SL - 1, 0.0, total_x[x + 1])
        grad[0, x] = -0.5 * (total + before + after)
        grad[1, x] = total_r[x]
        return carry

    lax.fori_loop(0, SL, gradients, 0)

    local[7].wait()
    first = lax.broadcasted_iota(jnp.int32, (256, LANES), 1) < 64
    cond_y = times_table(grad[0].reshape(256, NY), tabs[0])
    rate_y = times_table(grad[1].reshape(256, NY), tabs[0])
    for i in range(2):
        lanes = slice(i * LANES, (i + 1) * LANES)
        a = cond_y[:, lanes]
        b = pltpu.roll(rate_y[:, lanes], 64, 1)
        part[0, i] = jnp.where(first, a, b)
        part[1, i] = jnp.where(first, b, a)

    def to_mate(i, source, target):
        return pltpu.make_async_remote_copy(
            src_ref=source,
            dst_ref=target,
            send_sem=sum_send.at[i],
            recv_sem=sum_recv.at[i],
            device_id=(chip * 2 + 1 - core, space),
            device_id_type=MESH,
        )

    part_copy = to_mate(0, part.at[1 - core], part_in)
    part_copy.start()
    part_copy.wait_recv()
    for i in range(2):
        done = table_times(tabs[1], part[core, i] + part_in[i])
        column_out[i, :, 0:SL, :] = done.reshape(SP, SL, LANES)

    def none_faces(s, carry):
        for copy in conc_halo(s):
            copy.wait_recv()
        x_face(0, adj1, s, 0)
        x_face(0, adj1, s, SL)
        return carry

    lax.fori_loop(0, NSC, none_faces, 0)
    faces = jnp.concatenate([total_x[0], total_x[SL]], axis=0) * -0.5
    faces_y = times_table(faces, tabs[0])
    first_rim = lax.broadcasted_iota(jnp.int32, (NZ, LANES), 1) < 64
    for i in range(2):
        lanes = slice(i * LANES, (i + 1) * LANES)
        a = faces_y[0:NZ, lanes]
        b = pltpu.roll(faces_y[NZ : 2 * NZ, lanes], 64, 1)
        rim[0, i] = jnp.where(first_rim, a, b)
        rim[1, i] = jnp.where(first_rim, b, a)
    rim_copy = to_mate(1, rim.at[1 - core], rim_in)
    rim_copy.start()
    rim_copy.wait_recv()
    for i in range(2):
        done = table_times(tabs[3, :, 0:NZ, 0:NZ], rim[core, i] + rim_in[i])
        column_out[i, :, SL : SL + 1, :] = done.reshape(SP, 1, LANES)

    def column_copy(away, i):
        there = lax.rem(chip + away, 2)
        other = lax.rem(space + i, SP)
        return pltpu.make_async_remote_copy(
            src_ref=column_out.at[there, other],
            dst_ref=column.at[chip, space],
            send_sem=a2a_send.at[away, i],
            recv_sem=a2a_recv.at[away, i],
            device_id=(there * 2 + core, other),
            device_id_type=MESH,
        )

    def column_start(i, carry):
        column_copy(0, i).start()
        column_copy(1, i).start()
        return carry

    def column_wait(i, carry):
        column_copy(0, i).wait()
        column_copy(1, i).wait()
        return carry

    lax.fori_loop(1, SP, column_start, 0)
    column_copy(1, 0).start()
    column[chip, space] = column_out[chip, space]
    lax.fori_loop(1, SP, column_wait, 0)
    column_copy(1, 0).wait()
    both = column[0] + column[1]
    field_lanes = lax.broadcasted_iota(jnp.int32, (SP, 1, LANES), 2) // 64 == core
    edge = both[:, SL : SL + 1, :]
    lower = jnp.where(field_lanes, edge, 0.0)
    upper = jnp.where(field_lanes, pltpu.roll(edge.reshape(SP, LANES), 64, 1).reshape(SP, 1, LANES), 0.0)
    at_start = lower + jnp.concatenate([upper[SP - 1 :], upper[: SP - 1]], axis=0)
    at_end = upper + jnp.concatenate([lower[1:], lower[:1]], axis=0)
    place = lax.broadcasted_iota(jnp.int32, (SP, SL, LANES), 1)
    cells = both[:, 0:SL, :]
    cells = cells + jnp.where(place == 0, at_start, 0.0) + jnp.where(place == SL - 1, at_end, 0.0)

    spectral = table_times(tabs[0], cells.reshape(NX, LANES)) * spectrum[...]
    back_out[...] = table_times(tabs[0], spectral).reshape(SP, SL, LANES)

    def back_copy(i):
        other = lax.rem(space + i, SP)
        return pltpu.make_async_remote_copy(
            src_ref=back_out.at[other],
            dst_ref=back.at[space],
            send_sem=b2a_send.at[i],
            recv_sem=b2a_recv.at[i],
            device_id=(scen, other),
            device_id_type=MESH,
        )

    def back_start(i, carry):
        back_copy(i).start()
        return carry

    def back_wait(i, carry):
        back_copy(i).wait()
        return carry

    lax.fori_loop(1, SP, back_start, 0)
    back[space] = back_out[space]
    lax.fori_loop(1, SP, back_wait, 0)

    block_out[...] = table_times(tabs[2], back[...].reshape(256, LANES)).reshape(4, 64, LANES)
    block_copies = []
    for i in range(1, 4):
        other = lax.rem(scen + i, 4)
        block_copies.append(
            pltpu.make_async_remote_copy(
                src_ref=block_out.at[other],
                dst_ref=block.at[scen],
                send_sem=blk_send.at[i],
                recv_sem=blk_recv.at[i],
                device_id=(other, space),
                device_id_type=MESH,
            )
        )
    for copy in block_copies:
        copy.start()
    block[scen] = block_out[scen]
    for copy in cond_halo() + (part_copy, rim_copy):
        copy.wait_send()
    for s in range(NSC):
        for copy in adj_halo(s) + change_halo(s) + conc_halo(s):
            copy.wait_send()
    for copy in block_copies:
        copy.wait()

    first = lax.broadcasted_iota(jnp.int32, (64, LANES), 1) < 64
    cond_f = [jnp.where(first, block[i], block[i + 1]) for i in (0, 2)]
    rate_f = [pltpu.roll(jnp.where(first, block[i + 1], block[i]), 64, 1) for i in (0, 2)]
    for which, halves in enumerate((cond_f, rate_f)):
        whole = jnp.concatenate(halves, axis=1)
        out[which] = times_table(whole, tabs[0]).reshape(SL, 8, NY)


def body(states, terminal, log_cond, log_rate, well_cell, sample_step, well_misfit):
    hbm = pl.BlockSpec(memory_space=pl.ANY)
    smem = pl.BlockSpec(memory_space=pltpu.SMEM)
    vmem = pl.BlockSpec(memory_space=pltpu.VMEM)
    dma = pltpu.SemaphoreType.DMA
    slab = (SL, NZ, NY)
    scratch = [
        pltpu.VMEM((3, NSC, 3, SL + 2, NZ, NY), bf16),
        pltpu.VMEM((NSC, 3, SL + 2, NZ, NY), bf16),
        pltpu.VMEM((NSC, 3, SL + 2, NZ, NY), f32),
        pltpu.VMEM((NSC, 3, SL + 2, NZ, NY), f32),
        pltpu.VMEM((SL + 2, NZ, NY), f32),
        pltpu.VMEM(slab, f32),
        pltpu.VMEM((3, SL + 1, NZ, NY), f32),
        pltpu.VMEM((3,) + slab, f32),
        pltpu.VMEM((3,) + slab, f32),
        pltpu.VMEM((SL + 1, NZ, NY), f32),
        pltpu.VMEM(slab, f32),
        pltpu.VMEM(slab, f32),
        pltpu.VMEM(slab, f32),
        pltpu.VMEM((2, NSC, 3, NZ, NY), bf16),
        pltpu.VMEM((2, NSC, 3, NZ, NY), bf16),
        pltpu.VMEM((NSC, NW, 3), f32),
        pltpu.VMEM((NSC, SL + 2, NZ, 32), bf16),
        pltpu.VMEM((3, NSC, 3, 32, NY), bf16),
        pltpu.VMEM((4, 2, 256, 256), bf16),
        pltpu.VMEM((NX, LANES), f32),
        pltpu.VMEM((2,) + slab, f32),
        pltpu.VMEM((2, 2, 256, LANES), f32),
        pltpu.VMEM((2, 256, LANES), f32),
        pltpu.VMEM((2, 2, NZ, LANES), f32),
        pltpu.VMEM((2, NZ, LANES), f32),
        pltpu.VMEM((2, SP, SL + 1, LANES), f32),
        pltpu.VMEM((2, SP, SL + 1, LANES), f32),
        pltpu.VMEM((SP, SL, LANES), f32),
        pltpu.VMEM((SP, SL, LANES), f32),
        pltpu.VMEM((4, 64, LANES), f32),
        pltpu.VMEM((4, 64, LANES), f32),
        dma((8,)),
        dma((26,)),
        dma((26,)),
        dma((2,)),
        dma((2,)),
        dma((2, SP)),
        dma((2, SP)),
        dma((SP,)),
        dma((SP,)),
        dma((4,)),
        dma((4,)),
    ]
    return pl.pallas_call(
        kernel,
        out_shape=jax.ShapeDtypeStruct((2, SL, 8, NY), f32),
        in_specs=[hbm, hbm, hbm, hbm, smem, smem, hbm, hbm],
        out_specs=vmem,
        scratch_shapes=scratch,
        compiler_params=pltpu.CompilerParams(
            collective_id=0, has_side_effects=True, vmem_limit_bytes=60 * 1024 * 1024
        ),
    )(
        states,
        terminal,
        log_cond,
        log_rate,
        well_cell,
        sample_step,
        well_misfit,
        jnp.asarray(tables()),
    )


def solution(mesh):
    in_specs = (
        P(None, "scen", None, "space", None, None),
        P("scen", None, "space", None, None),
        P("space", None, None),
        P("space", None, None),
        P("scen", None),
        P("scen", None),
        P("scen", None, None),
    )
    out_specs = P(None, "space", "scen", None)
    return jax.shard_map(body, mesh=mesh, in_specs=in_specs, out_specs=out_specs, check_vma=False)
```

```python
import functools
import math

import jax
import jax.numpy as jnp
import numpy as np
from jax import lax
from jax.experimental import pallas as pl
from jax.experimental.pallas import tpu as pltpu
from jax.sharding import PartitionSpec as P

time_step = 0.05
diffusion = (1.0, 0.8, 0.1)
donor_half = 0.5
acceptor_half = 0.3
acceptor_yield = 0.5
biomass_yield = 0.4
lengths = (40.0, 24.0)
f32 = jnp.float32
bf16 = jnp.bfloat16
MESH = pl.DeviceIdType.MESH

SL = 8
NZ = 32
NY = 256
NSC = 4
NW = 8
SP = 32
NX = SL * SP
LANES = 128


def cas(rows, cols, count):
    angle = 2.0 * np.pi * (np.outer(rows, cols) % count) / count
    return np.cos(angle) + np.sin(angle)


def two_parts(table):
    high = table.astype(np.float32).astype(bf16)
    low = (table - high.astype(np.float64)).astype(np.float32).astype(bf16)
    return np.stack([high, low])


def tables():
    count = np.arange(256)
    line = cas(count, count, 256)
    small = cas(np.arange(NZ), np.arange(NZ), NZ)
    ahead = np.zeros((NZ, SL, SL, NZ))
    back = np.zeros((4, SL, 8, NZ, SL))
    for x in range(SL):
        ahead[:, x, x, :] = small
        back[:, x, :, :, x] = small.reshape(4, 8, NZ)
    corner = np.zeros((256, 256))
    corner[:NZ, :NZ] = small
    turned = [line, ahead.reshape(256, 256), back.reshape(256, 256), corner]
    return np.stack([two_parts(table) for table in turned])


def offsets_of(chips):
    found = []
    for away in range(chips):
        for i in range(SP):
            x, z, y = i // 8, i // 2 % 4, i % 2
            hops = min(x, 4 - x) + min(z, 4 - z) + (1 if away else 2 * y)
            if hops:
                found.append((-hops, i, away, (x, z, y)))
    return [(away, offset) for _, _, away, offset in sorted(found)]


def split2(value):
    high = value.astype(bf16)
    low = (value - high.astype(f32)).astype(bf16)
    return high, low


def mm(a, b):
    return jnp.dot(a, b, preferred_element_type=f32)


def table_times(table, data):
    high, low = split2(data)
    return mm(table[0], high) + mm(table[0], low) + mm(table[1], high)


def times_table(data, table):
    high, low = split2(data)
    return mm(high, table[0]) + mm(low, table[0]) + mm(high, table[1])


def kernel(
    states,
    terminal,
    log_cond,
    log_rate,
    well_cell,
    sample_step,
    well_misfit,
    tabs_hbm,
    out,
    conc,
    adj3,
    adj2,
    adj1,
    cond,
    rate,
    weight_x,
    weight_z,
    weight_y,
    total_x,
    total_z,
    total_y,
    total_r,
    change,
    change_in,
    hot,
    inject,
    tabs,
    spectrum,
    grad,
    part,
    part_in,
    rim,
    rim_in,
    column_out,
    column,
    back_out,
    back,
    block_out,
    block,
    local_sem,
    halo_send,
    halo_recv,
    sum_send,
    sum_recv,
    a2a_send,
    a2a_recv,
    b2a_send,
    b2a_recv,
    blk_send,
    blk_recv,
):
    scen = lax.axis_index("scen")
    space = lax.axis_index("space")
    chip = scen // 2
    core = lax.rem(scen, 2)
    left = lax.rem(space + SP - 1, SP)
    right = lax.rem(space + 1, SP)

    local = [
        pltpu.make_async_copy(terminal, adj3.at[:, :, 1 : 1 + SL], local_sem.at[0]),
        pltpu.make_async_copy(log_cond, cond.at[1 : 1 + SL], local_sem.at[1]),
        pltpu.make_async_copy(log_rate, rate, local_sem.at[2]),
        pltpu.make_async_copy(states.at[2], conc.at[2, :, :, 1 : 1 + SL], local_sem.at[3]),
        pltpu.make_async_copy(states.at[1], conc.at[1, :, :, 1 : 1 + SL], local_sem.at[4]),
        pltpu.make_async_copy(states.at[0], conc.at[0, :, :, 1 : 1 + SL], local_sem.at[5]),
        pltpu.make_async_copy(tabs_hbm, tabs, local_sem.at[6]),
    ]
    for copy in local:
        copy.start()

    part_x = [lax.rem(space // 8 + i, 4) * 8 for i in range(4)]
    part_z = [lax.rem(space // 2 + i, 4) * 2 for i in range(4)]
    part_y = [lax.rem(space + i, 2) for i in range(2)]
    on_chip = [chip * 2 + core, (1 - chip) * 2 + core]

    def other_of(offset):
        return part_x[offset[0]] + part_z[offset[1]] + part_y[offset[2]]

    barrier = pltpu.get_barrier_semaphore()

    def signal(to_scen, to_space):
        pl.semaphore_signal(
            barrier, inc=1, device_id=(to_scen, to_space), device_id_type=MESH
        )

    for away, offset in offsets_of(2):
        signal(on_chip[away], other_of(offset))
    signal(chip * 2 + 1 - core, space)
    signal((1 - chip) * 2 + 1 - core, space)
    pl.semaphore_wait(barrier, 2 * (SP - 1) + 3)

    def to_side(i, source, target, side):
        return pltpu.make_async_remote_copy(
            src_ref=source,
            dst_ref=target,
            send_sem=halo_send.at[i],
            recv_sem=halo_recv.at[i],
            device_id=(scen, side),
            device_id_type=MESH,
        )

    def cond_halo():
        return (
            to_side(0, log_cond.at[SL - 1], cond.at[0], right),
            to_side(1, log_cond.at[0], cond.at[SL + 1], left),
        )

    def adj_halo(s):
        return (
            to_side(2 + s, terminal.at[s, :, SL - 1], adj3.at[s, :, 0], right),
            to_side(6 + s, terminal.at[s, :, 0], adj3.at[s, :, SL + 1], left),
        )

    def change_halo(s):
        return (
            to_side(10 + s, change.at[1, s], change_in.at[0, s], right),
            to_side(14 + s, change.at[0, s], change_in.at[1, s], left),
        )

    def conc_halo(s):
        return (
            to_side(18 + s, states.at[0, s, :, SL - 1], conc.at[0, s, :, 0], right),
            to_side(22 + s, states.at[0, s, :, 0], conc.at[0, s, :, SL + 1], left),
        )

    for copy in cond_halo():
        copy.start()
    for s in range(NSC):
        for copy in adj_halo(s):
            copy.start()

    nothing = jnp.zeros((NZ, NY), f32)
    for s in range(NSC):
        for sp in range(3):
            for side in (0, SL + 1):
                conc[1, s, sp, side] = nothing.astype(bf16)
                conc[2, s, sp, side] = nothing.astype(bf16)
                adj1[s, sp, side] = nothing

    def clear(x, carry):
        total_x[x] = nothing
        total_z[x] = nothing
        total_y[x] = nothing
        total_r[x] = nothing
        return carry

    lax.fori_loop(0, SL, clear, 0)
    total_x[SL] = nothing

    local[1].wait()
    local[2].wait()
    z_index = lax.broadcasted_iota(jnp.int32, (NZ, NY), 0)
    y_index = lax.broadcasted_iota(jnp.int32, (NZ, NY), 1)

    def own_weights(x, carry):
        here = jnp.exp(cond[x])
        cond[x] = here
        rate[x - 1] = jnp.exp(rate[x - 1])
        above = jnp.sqrt(here * pltpu.roll(here, NZ - 1, 0))
        above = jnp.where(z_index == NZ - 1, 0.0, above)
        beside = jnp.sqrt(here * pltpu.roll(here, NY - 1, 1))
        beside = jnp.where(y_index == NY - 1, 0.0, beside)
        for sp in range(3):
            weight_z[sp, x - 1] = (time_step * diffusion[sp]) * above
            weight_y[sp, x - 1] = (time_step * diffusion[sp]) * beside
        return carry

    lax.fori_loop(1, SL + 1, own_weights, 0)

    def inner_weights(x, carry):
        between = jnp.sqrt(cond[x] * cond[x + 1])
        for sp in range(3):
            weight_x[sp, x] = (time_step * diffusion[sp]) * between
        return carry

    lax.fori_loop(1, SL, inner_weights, 0)

    lane = lax.broadcasted_iota(jnp.int32, (1, 32), 1)
    row_at = lax.broadcasted_iota(jnp.int32, (NZ, 32), 0)
    well_row = lax.broadcasted_iota(jnp.int32, (NW, NY), 0)
    well_col = lax.broadcasted_iota(jnp.int32, (NW, NY), 1)

    def wells(s, carry):
        row_of = jnp.full((1, 32), -1, jnp.int32)
        col_of = jnp.zeros((NW, NY), jnp.int32)
        step_of = jnp.zeros((NW, NY), jnp.int32)
        amounts = [jnp.zeros((NW, NY), f32)] * 3
        for w in range(NW):
            cell = well_cell[s, w]
            row = ((cell - space * (SL * NZ * NY)) >> 8) + NZ
            row_of = jnp.where(lane % NW == w, row, row_of)
            col_of = jnp.where(well_row == w, cell & 255, col_of)
            step_of = jnp.where(well_row == w, sample_step[s, w], step_of)
            amounts = [
                jnp.where(well_row == w, well_misfit[sp, s, w], amounts[sp]) for sp in range(3)
            ]
        row_of = jnp.where(lane < 3 * NW, row_of, -1)
        for x in range(SL + 2):
            hot[s, x] = jnp.where(row_at + x * NZ == row_of, 1.0, 0.0).astype(bf16)
        here = well_col == col_of
        for n in (1, 2):
            chosen = here & (step_of == n)
            for sp in range(3):
                value = jnp.where(chosen, amounts[sp], 0.0)
                high = value.astype(bf16).astype(f32)
                rest = value - high
                middle = rest.astype(bf16).astype(f32)
                low = rest - middle
                inject[n, s, sp] = jnp.concatenate(
                    [high, middle, low, jnp.zeros((NW, NY), f32)], axis=0
                ).astype(bf16)
        return carry

    lax.fori_loop(0, NSC, wells, 0)

    def x_flux(adj, s, sp, x):
        before = adj[s, sp, x].astype(f32)
        return weight_x[sp, x] * (adj[s, sp, x + 1].astype(f32) - before)

    def layer(n, adj, new, s, x, side=None, face=True):
        own = x - 1
        conc_here = [conc[n, s, sp, x].astype(f32) for sp in range(3)]
        adj_here = [adj[s, sp, x].astype(f32) for sp in range(3)]
        sum_x = total_x[x]
        sum_z = total_z[own]
        sum_y = total_y[own]
        spread = []
        for sp in range(3):
            a, c = adj_here[sp], conc_here[sp]
            flux_z = weight_z[sp, own] * (pltpu.roll(a, NZ - 1, 0) - a)
            flux_y = weight_y[sp, own] * (pltpu.roll(a, NY - 1, 1) - a)
            sum_z = sum_z + (pltpu.roll(c, NZ - 1, 0) - c) * flux_z
            sum_y = sum_y + (pltpu.roll(c, NY - 1, 1) - c) * flux_y
            if face:
                flux_x = x_flux(adj, s, sp, x)
                sum_x = sum_x + (conc[n, s, sp, x + 1].astype(f32) - c) * flux_x
            if new is not None:
                spread.append(
                    (flux_x - x_flux(adj, s, sp, x - 1))
                    + (flux_z - pltpu.roll(flux_z, 1, 0))
                    + (flux_y - pltpu.roll(flux_y, 1, 1))
                )
        if face:
            total_x[x] = sum_x
        total_z[own] = sum_z
        total_y[own] = sum_y
        donor, acceptor, biomass = conc_here
        donor_inv = 1.0 / (donor_half + donor)
        accept_inv = 1.0 / (acceptor_half + acceptor)
        donor_mono = donor * donor_inv
        accept_mono = acceptor * accept_inv
        both = donor_mono * accept_mono
        stoich = -adj_here[0] - acceptor_yield * adj_here[1] + biomass_yield * adj_here[2]
        scaled = (time_step * stoich) * rate[own]
        growth = scaled * biomass
        total_r[own] = total_r[own] + growth * both
        if new is None:
            return
        spread[0] = spread[0] + (growth * accept_mono) * (donor_half * (donor_inv * donor_inv))
        spread[1] = spread[1] + (growth * donor_mono) * (acceptor_half * (accept_inv * accept_inv))
        spread[2] = spread[2] + scaled * both
        rows = hot[s, x]
        for sp in range(3):
            if side is not None:
                change[side, s, sp] = spread[sp].astype(bf16)
            new[s, sp, x] = adj_here[sp] + spread[sp] + mm(rows, inject[n, s, sp])

    def x_face(n, adj, s, x):
        total = total_x[x]
        for sp in range(3):
            step_c = conc[n, s, sp, x + 1].astype(f32) - conc[n, s, sp, x].astype(f32)
            total = total + step_c * x_flux(adj, s, sp, x)
        total_x[x] = total

    def layers(n, adj, new, s, first, last):
        def one(x, carry):
            layer(n, adj, new, s, x)
            return carry

        lax.fori_loop(first, last, one, 0)

    local[0].wait()
    local[3].wait()

    def inner_two(s, carry):
        layers(2, adj3, adj2, s, 2, SL)
        return carry

    lax.fori_loop(0, NSC, inner_two, 0)
    for copy in cond_halo():
        copy.wait_recv()
    for x, beyond, wall in ((0, 0, space == 0), (SL, SL + 1, space == SP - 1)):
        between = jnp.sqrt(jnp.exp(cond[beyond]) * cond[2 * x + 1 - beyond])
        between = jnp.where(wall, 0.0, between)
        for sp in range(3):
            weight_x[sp, x] = (time_step * diffusion[sp]) * between
    local[4].wait()

    def two_and_one(s, carry):
        for copy in adj_halo(s):
            copy.wait_recv()
        layer(2, adj3, adj2, s, 1, 0)
        layer(2, adj3, adj2, s, SL, 1)
        for copy in change_halo(s):
            copy.start()
        x_face(2, adj3, s, 0)
        layers(1, adj2, adj1, s, 2, SL)
        return carry

    lax.fori_loop(0, NSC, two_and_one, 0)
    row = lax.broadcasted_iota(jnp.int32, (NX, LANES), 0)
    col = lax.broadcasted_iota(jnp.int32, (NX, LANES), 1)
    wave_x = jnp.minimum(row, NX - row).astype(f32) * (2.0 * math.pi / NX)
    freq_y = scen * 64 + col % 64
    wave_y = jnp.minimum(freq_y, NY - freq_y).astype(f32) * (2.0 * math.pi / NY)
    freq_z = jnp.full((1, LANES), space, jnp.int32)
    wave_z = jnp.minimum(freq_z, NZ - freq_z).astype(f32) * (2.0 * math.pi / NZ)
    field = (col // 64 + scen) % 2
    length = jnp.where(field == 0, lengths[0], lengths[1])
    square = wave_x * wave_x + wave_z * wave_z + wave_y * wave_y
    spectrum[...] = (length / jnp.sqrt(1.0 + (length * length) * square)) * (1.0 / (NX * NZ * NY))
    local[5].wait()

    def one_and_none(s, carry):
        for copy in change_halo(s):
            copy.wait_recv()
        for side, x in ((0, 0), (1, SL + 1)):
            rows = hot[s, x]
            for sp in range(3):
                adj2[s, sp, x] = (
                    adj3[s, sp, x].astype(f32)
                    + change_in[side, s, sp].astype(f32)
                    + mm(rows, inject[2, s, sp])
                )
        for copy in conc_halo(s):
            copy.start()
        layer(1, adj2, adj1, s, 1)
        layer(1, adj2, adj1, s, SL)
        x_face(1, adj2, s, 0)
        layers(0, adj1, None, s, 1, SL)
        layer(0, adj1, None, s, SL, face=False)
        return carry

    lax.fori_loop(0, NSC, one_and_none, 0)

    def gradients(x, carry):
        along_z = total_z[x]
        along_y = total_y[x]
        total = along_z + pltpu.roll(along_z, 1, 0) + along_y + pltpu.roll(along_y, 1, 1)
        before = jnp.where(x == 0, 0.0, total_x[x])
        after = jnp.where(x == SL - 1, 0.0, total_x[x + 1])
        grad[0, x] = -0.5 * (total + before + after)
        grad[1, x] = total_r[x]
        return carry

    lax.fori_loop(0, SL, gradients, 0)

    local[6].wait()
    first = lax.broadcasted_iota(jnp.int32, (256, LANES), 1) < 64
    cond_y = times_table(grad[0].reshape(256, NY), tabs[0])
    rate_y = times_table(grad[1].reshape(256, NY), tabs[0])
    for i in range(2):
        lanes = slice(i * LANES, (i + 1) * LANES)
        a = cond_y[:, lanes]
        b = pltpu.roll(rate_y[:, lanes], 64, 1)
        part[0, i] = jnp.where(first, a, b)
        part[1, i] = jnp.where(first, b, a)

    def to_mate(i, source, target):
        return pltpu.make_async_remote_copy(
            src_ref=source,
            dst_ref=target,
            send_sem=sum_send.at[i],
            recv_sem=sum_recv.at[i],
            device_id=(chip * 2 + 1 - core, space),
            device_id_type=MESH,
        )

    part_copy = to_mate(0, part.at[1 - core], part_in)
    part_copy.start()
    part_copy.wait_recv()
    for i in range(2):
        done = table_times(tabs[1], part[core, i] + part_in[i])
        column_out[i, :, 0:SL, :] = done.reshape(SP, SL, LANES)

    def none_faces(s, carry):
        for copy in conc_halo(s):
            copy.wait_recv()
        x_face(0, adj1, s, 0)
        x_face(0, adj1, s, SL)
        return carry

    lax.fori_loop(0, NSC, none_faces, 0)
    faces = jnp.concatenate([total_x[0], total_x[SL]], axis=0) * -0.5
    faces_y = times_table(faces, tabs[0])
    first_rim = lax.broadcasted_iota(jnp.int32, (NZ, LANES), 1) < 64
    for i in range(2):
        lanes = slice(i * LANES, (i + 1) * LANES)
        a = faces_y[0:NZ, lanes]
        b = pltpu.roll(faces_y[NZ : 2 * NZ, lanes], 64, 1)
        rim[0, i] = jnp.where(first_rim, a, b)
        rim[1, i] = jnp.where(first_rim, b, a)
    rim_copy = to_mate(1, rim.at[1 - core], rim_in)
    rim_copy.start()
    rim_copy.wait_recv()
    for i in range(2):
        done = table_times(tabs[3, :, 0:NZ, 0:NZ], rim[core, i] + rim_in[i])
        column_out[i, :, SL : SL + 1, :] = done.reshape(SP, 1, LANES)

    column_copies = []
    for i, (away, offset) in enumerate(offsets_of(2)):
        there = chip if away == 0 else 1 - chip
        other = other_of(offset)
        column_copies.append(
            pltpu.make_async_remote_copy(
                src_ref=column_out.at[there, other],
                dst_ref=column.at[chip, space],
                send_sem=a2a_send.at[i],
                recv_sem=a2a_recv.at[i],
                device_id=(on_chip[away], other),
                device_id_type=MESH,
            )
        )
    for copy in column_copies:
        copy.start()
    column[chip, space] = column_out[chip, space]
    for copy in column_copies:
        copy.wait_recv()
    both = column[0] + column[1]
    field_lanes = lax.broadcasted_iota(jnp.int32, (SP, 1, LANES), 2) // 64 == core
    edge = both[:, SL : SL + 1, :]
    lower = jnp.where(field_lanes, edge, 0.0)
    upper = jnp.where(field_lanes, pltpu.roll(edge.reshape(SP, LANES), 64, 1).reshape(SP, 1, LANES), 0.0)
    at_start = lower + jnp.concatenate([upper[SP - 1 :], upper[: SP - 1]], axis=0)
    at_end = upper + jnp.concatenate([lower[1:], lower[:1]], axis=0)
    place = lax.broadcasted_iota(jnp.int32, (SP, SL, LANES), 1)
    cells = both[:, 0:SL, :]
    cells = cells + jnp.where(place == 0, at_start, 0.0) + jnp.where(place == SL - 1, at_end, 0.0)

    spectral = table_times(tabs[0], cells.reshape(NX, LANES)) * spectrum[...]
    back_out[...] = table_times(tabs[0], spectral).reshape(SP, SL, LANES)

    back_copies = []
    for i, (_, offset) in enumerate(offsets_of(1)):
        other = other_of(offset)
        back_copies.append(
            pltpu.make_async_remote_copy(
                src_ref=back_out.at[other],
                dst_ref=back.at[space],
                send_sem=b2a_send.at[i],
                recv_sem=b2a_recv.at[i],
                device_id=(scen, other),
                device_id_type=MESH,
            )
        )
    for copy in back_copies:
        copy.start()
    back[space] = back_out[space]
    for copy in back_copies:
        copy.wait_recv()

    block_out[...] = table_times(tabs[2], back[...].reshape(256, LANES)).reshape(4, 64, LANES)
    block_copies = []
    for i in range(1, 4):
        other = lax.rem(scen + i, 4)
        block_copies.append(
            pltpu.make_async_remote_copy(
                src_ref=block_out.at[other],
                dst_ref=block.at[scen],
                send_sem=blk_send.at[i],
                recv_sem=blk_recv.at[i],
                device_id=(other, space),
                device_id_type=MESH,
            )
        )
    for copy in block_copies:
        copy.start()
    block[scen] = block_out[scen]
    for copy in cond_halo() + (part_copy, rim_copy):
        copy.wait_send()
    for copy in column_copies + back_copies:
        copy.wait_send()
    for s in range(NSC):
        for copy in adj_halo(s) + change_halo(s) + conc_halo(s):
            copy.wait_send()
    for copy in block_copies:
        copy.wait()

    first = lax.broadcasted_iota(jnp.int32, (64, LANES), 1) < 64
    cond_f = [jnp.where(first, block[i], block[i + 1]) for i in (0, 2)]
    rate_f = [pltpu.roll(jnp.where(first, block[i + 1], block[i]), 64, 1) for i in (0, 2)]
    for which, halves in enumerate((cond_f, rate_f)):
        whole = jnp.concatenate(halves, axis=1)
        out[which] = times_table(whole, tabs[0]).reshape(SL, 8, NY)


def body(states, terminal, log_cond, log_rate, well_cell, sample_step, well_misfit):
    hbm = pl.BlockSpec(memory_space=pl.ANY)
    smem = pl.BlockSpec(memory_space=pltpu.SMEM)
    vmem = pl.BlockSpec(memory_space=pltpu.VMEM)
    dma = pltpu.SemaphoreType.DMA
    slab = (SL, NZ, NY)
    scratch = [
        pltpu.VMEM((3, NSC, 3, SL + 2, NZ, NY), bf16),
        pltpu.VMEM((NSC, 3, SL + 2, NZ, NY), bf16),
        pltpu.VMEM((NSC, 3, SL + 2, NZ, NY), f32),
        pltpu.VMEM((NSC, 3, SL + 2, NZ, NY), f32),
        pltpu.VMEM((SL + 2, NZ, NY), f32),
        pltpu.VMEM(slab, f32),
        pltpu.VMEM((3, SL + 1, NZ, NY), f32),
        pltpu.VMEM((3,) + slab, f32),
        pltpu.VMEM((3,) + slab, f32),
        pltpu.VMEM((SL + 1, NZ, NY), f32),
        pltpu.VMEM(slab, f32),
        pltpu.VMEM(slab, f32),
        pltpu.VMEM(slab, f32),
        pltpu.VMEM((2, NSC, 3, NZ, NY), bf16),
        pltpu.VMEM((2, NSC, 3, NZ, NY), bf16),
        pltpu.VMEM((NSC, SL + 2, NZ, 32), bf16),
        pltpu.VMEM((3, NSC, 3, 32, NY), bf16),
        pltpu.VMEM((4, 2, 256, 256), bf16),
        pltpu.VMEM((NX, LANES), f32),
        pltpu.VMEM((2,) + slab, f32),
        pltpu.VMEM((2, 2, 256, LANES), f32),
        pltpu.VMEM((2, 256, LANES), f32),
        pltpu.VMEM((2, 2, NZ, LANES), f32),
        pltpu.VMEM((2, NZ, LANES), f32),
        pltpu.VMEM((2, SP, SL + 1, LANES), f32),
        pltpu.VMEM((2, SP, SL + 1, LANES), f32),
        pltpu.VMEM((SP, SL, LANES), f32),
        pltpu.VMEM((SP, SL, LANES), f32),
        pltpu.VMEM((4, 64, LANES), f32),
        pltpu.VMEM((4, 64, LANES), f32),
        dma((7,)),
        dma((26,)),
        dma((26,)),
        dma((2,)),
        dma((2,)),
        dma((2 * SP - 1,)),
        dma((2 * SP - 1,)),
        dma((SP - 1,)),
        dma((SP - 1,)),
        dma((4,)),
        dma((4,)),
    ]
    return pl.pallas_call(
        kernel,
        out_shape=jax.ShapeDtypeStruct((2, SL, 8, NY), f32),
        in_specs=[hbm, hbm, hbm, hbm, smem, smem, smem, hbm],
        out_specs=vmem,
        scratch_shapes=scratch,
        compiler_params=pltpu.CompilerParams(
            collective_id=0, has_side_effects=True, vmem_limit_bytes=60 * 1024 * 1024
        ),
    )(
        states,
        terminal,
        log_cond,
        log_rate,
        well_cell,
        sample_step,
        jnp.transpose(well_misfit, (2, 0, 1)),
        jnp.asarray(tables()),
    )


def solution(mesh):
    in_specs = (
        P(None, "scen", None, "space", None, None),
        P("scen", None, "space", None, None),
        P("space", None, None),
        P("space", None, None),
        P("scen", None),
        P("scen", None),
        P("scen", None, None),
    )
    out_specs = P(None, "space", "scen", None)
    return jax.shard_map(body, mesh=mesh, in_specs=in_specs, out_specs=out_specs, check_vma=False)
```

```python
import functools
import math

import jax
import jax.numpy as jnp
import numpy as np
from jax import lax
from jax.experimental import pallas as pl
from jax.experimental.pallas import tpu as pltpu
from jax.sharding import PartitionSpec as P

time_step = 0.05
diffusion = (1.0, 0.8, 0.1)
donor_half = 0.5
acceptor_half = 0.3
acceptor_yield = 0.5
biomass_yield = 0.4
lengths = (40.0, 24.0)
f32 = jnp.float32
bf16 = jnp.bfloat16
MESH = pl.DeviceIdType.MESH

SL = 8
NZ = 32
NY = 256
NSC = 4
NW = 8
SP = 32
NX = SL * SP
LANES = 128


def cas(rows, cols, count):
    angle = 2.0 * np.pi * (np.outer(rows, cols) % count) / count
    return np.cos(angle) + np.sin(angle)


def two_parts(table):
    high = table.astype(np.float32).astype(bf16)
    low = (table - high.astype(np.float64)).astype(np.float32).astype(bf16)
    return np.stack([high, low])


def tables():
    count = np.arange(256)
    line = cas(count, count, 256)
    small = cas(np.arange(NZ), np.arange(NZ), NZ)
    ahead = np.zeros((NZ, SL, SL, NZ))
    back = np.zeros((4, SL, 8, NZ, SL))
    for x in range(SL):
        ahead[:, x, x, :] = small
        back[:, x, :, :, x] = small.reshape(4, 8, NZ)
    corner = np.zeros((256, 256))
    corner[:NZ, :NZ] = small
    turned = [line, ahead.reshape(256, 256), back.reshape(256, 256), corner]
    return np.stack([two_parts(table) for table in turned])


def offsets_of(chips):
    found = []
    for away in range(chips):
        for i in range(SP):
            x, z, y = i // 8, i // 2 % 4, i % 2
            hops = min(x, 4 - x) + min(z, 4 - z) + (1 if away else 2 * y)
            if hops:
                found.append((-hops, i, away, (x, z, y)))
    return [(away, offset) for _, _, away, offset in sorted(found)]


def split2(value):
    high = value.astype(bf16)
    low = (value - high.astype(f32)).astype(bf16)
    return high, low


def mm(a, b):
    return jnp.dot(a, b, preferred_element_type=f32)


def table_times(table, data):
    high, low = split2(data)
    return mm(table[0], high) + mm(table[0], low) + mm(table[1], high)


def times_table(data, table):
    high, low = split2(data)
    return mm(high, table[0]) + mm(low, table[0]) + mm(high, table[1])


def kernel(
    states,
    terminal,
    log_cond,
    log_rate,
    well_cell,
    sample_step,
    well_misfit,
    tabs_hbm,
    out,
    conc,
    adj3,
    adj2,
    adj1,
    cond,
    rate,
    weight_x,
    weight_z,
    weight_y,
    total_x,
    total_z,
    total_y,
    total_r,
    change,
    change_in,
    hot,
    inject,
    tabs,
    spectrum,
    grad,
    part,
    part_in,
    rim,
    rim_in,
    column_out,
    column,
    back_out,
    back,
    block_out,
    block,
    local_sem,
    halo_send,
    halo_recv,
    sum_send,
    sum_recv,
    a2a_send,
    a2a_recv,
    b2a_send,
    b2a_recv,
    blk_send,
    blk_recv,
):
    scen = lax.axis_index("scen")
    space = lax.axis_index("space")
    chip = scen // 2
    core = lax.rem(scen, 2)
    left = lax.rem(space + SP - 1, SP)
    right = lax.rem(space + 1, SP)

    local = [
        pltpu.make_async_copy(terminal, adj3.at[:, :, 1 : 1 + SL], local_sem.at[0]),
        pltpu.make_async_copy(log_cond, cond.at[1 : 1 + SL], local_sem.at[1]),
        pltpu.make_async_copy(log_rate, rate, local_sem.at[2]),
        pltpu.make_async_copy(states.at[2], conc.at[2, :, :, 1 : 1 + SL], local_sem.at[3]),
        pltpu.make_async_copy(states.at[1], conc.at[1, :, :, 1 : 1 + SL], local_sem.at[4]),
        pltpu.make_async_copy(states.at[0], conc.at[0, :, :, 1 : 1 + SL], local_sem.at[5]),
        pltpu.make_async_copy(tabs_hbm, tabs, local_sem.at[6]),
    ]
    for copy in local:
        copy.start()

    part_x = [lax.rem(space // 8 + i, 4) * 8 for i in range(4)]
    part_z = [lax.rem(space // 2 + i, 4) * 2 for i in range(4)]
    part_y = [lax.rem(space + i, 2) for i in range(2)]
    on_chip = [chip * 2 + core, (1 - chip) * 2 + core]

    def other_of(offset):
        return part_x[offset[0]] + part_z[offset[1]] + part_y[offset[2]]

    barrier = pltpu.get_barrier_semaphore()

    def signal(to_scen, to_space):
        pl.semaphore_signal(
            barrier, inc=1, device_id=(to_scen, to_space), device_id_type=MESH
        )

    for away, offset in offsets_of(2):
        signal(on_chip[away], other_of(offset))
    signal(chip * 2 + 1 - core, space)
    signal((1 - chip) * 2 + 1 - core, space)
    pl.semaphore_wait(barrier, 2 * (SP - 1) + 3)

    def to_side(i, source, target, side):
        return pltpu.make_async_remote_copy(
            src_ref=source,
            dst_ref=target,
            send_sem=halo_send.at[i],
            recv_sem=halo_recv.at[i],
            device_id=(scen, side),
            device_id_type=MESH,
        )

    def cond_halo():
        return (
            to_side(0, log_cond.at[SL - 1], cond.at[0], right),
            to_side(1, log_cond.at[0], cond.at[SL + 1], left),
        )

    def adj_halo(s):
        return (
            to_side(2 + s, terminal.at[s, :, SL - 1], adj3.at[s, :, 0], right),
            to_side(6 + s, terminal.at[s, :, 0], adj3.at[s, :, SL + 1], left),
        )

    def change_halo(s):
        return (
            to_side(10 + s, change.at[1, s], change_in.at[0, s], right),
            to_side(14 + s, change.at[0, s], change_in.at[1, s], left),
        )

    def conc_halo(s):
        return (
            to_side(18 + s, states.at[0, s, :, SL - 1], conc.at[0, s, :, 0], right),
            to_side(22 + s, states.at[0, s, :, 0], conc.at[0, s, :, SL + 1], left),
        )

    for copy in cond_halo():
        copy.start()
    for s in range(NSC):
        for copy in adj_halo(s):
            copy.start()

    nothing = jnp.zeros((NZ, NY), f32)
    for s in range(NSC):
        for sp in range(3):
            for side in (0, SL + 1):
                conc[1, s, sp, side] = nothing.astype(bf16)
                conc[2, s, sp, side] = nothing.astype(bf16)
                adj1[s, sp, side] = nothing

    def clear(x, carry):
        total_x[x] = nothing
        total_z[x] = nothing
        total_y[x] = nothing
        total_r[x] = nothing
        return carry

    lax.fori_loop(0, SL, clear, 0)
    total_x[SL] = nothing

    local[1].wait()
    local[2].wait()
    z_index = lax.broadcasted_iota(jnp.int32, (NZ, NY), 0)
    y_index = lax.broadcasted_iota(jnp.int32, (NZ, NY), 1)

    def own_weights(x, carry):
        here = jnp.exp(cond[x])
        cond[x] = here
        rate[x - 1] = jnp.exp(rate[x - 1])
        above = jnp.sqrt(here * pltpu.roll(here, NZ - 1, 0))
        above = jnp.where(z_index == NZ - 1, 0.0, above)
        beside = jnp.sqrt(here * pltpu.roll(here, NY - 1, 1))
        beside = jnp.where(y_index == NY - 1, 0.0, beside)
        for sp in range(3):
            weight_z[sp, x - 1] = (time_step * diffusion[sp]) * above
            weight_y[sp, x - 1] = (time_step * diffusion[sp]) * beside
        return carry

    lax.fori_loop(1, SL + 1, own_weights, 0)

    def inner_weights(x, carry):
        between = jnp.sqrt(cond[x] * cond[x + 1])
        for sp in range(3):
            weight_x[sp, x] = (time_step * diffusion[sp]) * between
        return carry

    lax.fori_loop(1, SL, inner_weights, 0)

    lane = lax.broadcasted_iota(jnp.int32, (1, 32), 1)
    row_at = lax.broadcasted_iota(jnp.int32, (NZ, 32), 0)
    well_row = lax.broadcasted_iota(jnp.int32, (NW, NY), 0)
    well_col = lax.broadcasted_iota(jnp.int32, (NW, NY), 1)

    def wells(s, carry):
        row_of = jnp.full((1, 32), -1, jnp.int32)
        col_of = jnp.zeros((NW, NY), jnp.int32)
        step_of = jnp.zeros((NW, NY), jnp.int32)
        amounts = [jnp.zeros((NW, NY), f32)] * 3
        for w in range(NW):
            cell = well_cell[s, w]
            row = ((cell - space * (SL * NZ * NY)) >> 8) + NZ
            row_of = jnp.where(lane % NW == w, row, row_of)
            col_of = jnp.where(well_row == w, cell & 255, col_of)
            step_of = jnp.where(well_row == w, sample_step[s, w], step_of)
            amounts = [
                jnp.where(well_row == w, well_misfit[sp, s, w], amounts[sp]) for sp in range(3)
            ]
        row_of = jnp.where(lane < 3 * NW, row_of, -1)
        for x in range(SL + 2):
            hot[s, x] = jnp.where(row_at + x * NZ == row_of, 1.0, 0.0).astype(bf16)
        here = well_col == col_of
        for n in (1, 2):
            chosen = here & (step_of == n)
            for sp in range(3):
                value = jnp.where(chosen, amounts[sp], 0.0)
                high = value.astype(bf16).astype(f32)
                rest = value - high
                middle = rest.astype(bf16).astype(f32)
                low = rest - middle
                inject[n, s, sp] = jnp.concatenate(
                    [high, middle, low, jnp.zeros((NW, NY), f32)], axis=0
                ).astype(bf16)
        return carry

    lax.fori_loop(0, NSC, wells, 0)

    def x_flux(adj, s, sp, x):
        before = adj[s, sp, x].astype(f32)
        return weight_x[sp, x] * (adj[s, sp, x + 1].astype(f32) - before)

    def layer(n, adj, new, s, x, side=None, face=True):
        own = x - 1
        conc_here = [conc[n, s, sp, x].astype(f32) for sp in range(3)]
        adj_here = [adj[s, sp, x].astype(f32) for sp in range(3)]
        sum_x = total_x[x]
        sum_z = total_z[own]
        sum_y = total_y[own]
        spread = []
        for sp in range(3):
            a, c = adj_here[sp], conc_here[sp]
            flux_z = weight_z[sp, own] * (pltpu.roll(a, NZ - 1, 0) - a)
            flux_y = weight_y[sp, own] * (pltpu.roll(a, NY - 1, 1) - a)
            sum_z = sum_z + (pltpu.roll(c, NZ - 1, 0) - c) * flux_z
            sum_y = sum_y + (pltpu.roll(c, NY - 1, 1) - c) * flux_y
            if face:
                flux_x = x_flux(adj, s, sp, x)
                sum_x = sum_x + (conc[n, s, sp, x + 1].astype(f32) - c) * flux_x
            if new is not None:
                spread.append(
                    (flux_x - x_flux(adj, s, sp, x - 1))
                    + (flux_z - pltpu.roll(flux_z, 1, 0))
                    + (flux_y - pltpu.roll(flux_y, 1, 1))
                )
        if face:
            total_x[x] = sum_x
        total_z[own] = sum_z
        total_y[own] = sum_y
        donor, acceptor, biomass = conc_here
        donor_inv = 1.0 / (donor_half + donor)
        accept_inv = 1.0 / (acceptor_half + acceptor)
        donor_mono = donor * donor_inv
        accept_mono = acceptor * accept_inv
        both = donor_mono * accept_mono
        stoich = -adj_here[0] - acceptor_yield * adj_here[1] + biomass_yield * adj_here[2]
        scaled = (time_step * stoich) * rate[own]
        growth = scaled * biomass
        total_r[own] = total_r[own] + growth * both
        if new is None:
            return
        spread[0] = spread[0] + (growth * accept_mono) * (donor_half * (donor_inv * donor_inv))
        spread[1] = spread[1] + (growth * donor_mono) * (acceptor_half * (accept_inv * accept_inv))
        spread[2] = spread[2] + scaled * both
        rows = hot[s, x]
        for sp in range(3):
            if side is not None:
                change[side, s, sp] = spread[sp].astype(bf16)
            new[s, sp, x] = adj_here[sp] + spread[sp] + mm(rows, inject[n, s, sp])

    def x_face(n, adj, s, x):
        total = total_x[x]
        for sp in range(3):
            step_c = conc[n, s, sp, x + 1].astype(f32) - conc[n, s, sp, x].astype(f32)
            total = total + step_c * x_flux(adj, s, sp, x)
        total_x[x] = total

    def layers(n, adj, new, s, first, last):
        def one(x, carry):
            layer(n, adj, new, s, x)
            return carry

        lax.fori_loop(first, last, one, 0)

    local[0].wait()
    local[3].wait()

    def inner_two(s, carry):
        layers(2, adj3, adj2, s, 2, SL)
        return carry

    lax.fori_loop(0, NSC, inner_two, 0)
    for copy in cond_halo():
        copy.wait_recv()
    for x, beyond, wall in ((0, 0, space == 0), (SL, SL + 1, space == SP - 1)):
        between = jnp.sqrt(jnp.exp(cond[beyond]) * cond[2 * x + 1 - beyond])
        between = jnp.where(wall, 0.0, between)
        for sp in range(3):
            weight_x[sp, x] = (time_step * diffusion[sp]) * between
    local[4].wait()

    def two_and_one(s, carry):
        for copy in adj_halo(s):
            copy.wait_recv()
        layer(2, adj3, adj2, s, 1, 0)
        layer(2, adj3, adj2, s, SL, 1)
        for copy in change_halo(s):
            copy.start()
        x_face(2, adj3, s, 0)
        layers(1, adj2, adj1, s, 2, SL)
        return carry

    lax.fori_loop(0, NSC, two_and_one, 0)
    row = lax.broadcasted_iota(jnp.int32, (NX, LANES), 0)
    col = lax.broadcasted_iota(jnp.int32, (NX, LANES), 1)
    wave_x = jnp.minimum(row, NX - row).astype(f32) * (2.0 * math.pi / NX)
    freq_y = scen * 64 + col % 64
    wave_y = jnp.minimum(freq_y, NY - freq_y).astype(f32) * (2.0 * math.pi / NY)
    freq_z = jnp.full((1, LANES), space, jnp.int32)
    wave_z = jnp.minimum(freq_z, NZ - freq_z).astype(f32) * (2.0 * math.pi / NZ)
    field = (col // 64 + scen) % 2
    length = jnp.where(field == 0, lengths[0], lengths[1])
    square = wave_x * wave_x + wave_z * wave_z + wave_y * wave_y
    spectrum[...] = (length / jnp.sqrt(1.0 + (length * length) * square)) * (1.0 / (NX * NZ * NY))
    local[5].wait()

    def one_and_none(s, carry):
        for copy in change_halo(s):
            copy.wait_recv()
        for side, x in ((0, 0), (1, SL + 1)):
            rows = hot[s, x]
            for sp in range(3):
                adj2[s, sp, x] = (
                    adj3[s, sp, x].astype(f32)
                    + change_in[side, s, sp].astype(f32)
                    + mm(rows, inject[2, s, sp])
                )
        for copy in conc_halo(s):
            copy.start()
        layer(1, adj2, adj1, s, 1)
        layer(1, adj2, adj1, s, SL)
        x_face(1, adj2, s, 0)
        layers(0, adj1, None, s, 1, SL)
        layer(0, adj1, None, s, SL, face=False)
        return carry

    lax.fori_loop(0, NSC, one_and_none, 0)

    def gradients(x, carry):
        along_z = total_z[x]
        along_y = total_y[x]
        total = along_z + pltpu.roll(along_z, 1, 0) + along_y + pltpu.roll(along_y, 1, 1)
        before = jnp.where(x == 0, 0.0, total_x[x])
        after = jnp.where(x == SL - 1, 0.0, total_x[x + 1])
        grad[0, x] = -0.5 * (total + before + after)
        grad[1, x] = total_r[x]
        return carry

    lax.fori_loop(0, SL, gradients, 0)

    local[6].wait()
    first = lax.broadcasted_iota(jnp.int32, (256, LANES), 1) < 64
    cond_y = times_table(grad[0].reshape(256, NY), tabs[0])
    rate_y = times_table(grad[1].reshape(256, NY), tabs[0])
    for i in range(2):
        lanes = slice(i * LANES, (i + 1) * LANES)
        a = cond_y[:, lanes]
        b = pltpu.roll(rate_y[:, lanes], 64, 1)
        part[0, i] = jnp.where(first, a, b)
        part[1, i] = jnp.where(first, b, a)

    def to_mate(i, source, target):
        return pltpu.make_async_remote_copy(
            src_ref=source,
            dst_ref=target,
            send_sem=sum_send.at[i],
            recv_sem=sum_recv.at[i],
            device_id=(chip * 2 + 1 - core, space),
            device_id_type=MESH,
        )

    part_copy = to_mate(0, part.at[1 - core], part_in)
    part_copy.start()
    part_copy.wait_recv()
    for i in range(2):
        done = table_times(tabs[1], part[core, i] + part_in[i])
        column_out[i, :, 0:SL, :] = done.reshape(SP, SL, LANES)

    def none_faces(s, carry):
        for copy in conc_halo(s):
            copy.wait_recv()
        x_face(0, adj1, s, 0)
        x_face(0, adj1, s, SL)
        return carry

    lax.fori_loop(0, NSC, none_faces, 0)
    faces = jnp.concatenate([total_x[0], total_x[SL]], axis=0) * -0.5
    faces_y = times_table(faces, tabs[0])
    first_rim = lax.broadcasted_iota(jnp.int32, (NZ, LANES), 1) < 64
    for i in range(2):
        lanes = slice(i * LANES, (i + 1) * LANES)
        a = faces_y[0:NZ, lanes]
        b = pltpu.roll(faces_y[NZ : 2 * NZ, lanes], 64, 1)
        rim[0, i] = jnp.where(first_rim, a, b)
        rim[1, i] = jnp.where(first_rim, b, a)
    rim_copy = to_mate(1, rim.at[1 - core], rim_in)
    rim_copy.start()
    rim_copy.wait_recv()
    for i in range(2):
        done = table_times(tabs[3, :, 0:NZ, 0:NZ], rim[core, i] + rim_in[i])
        column_out[i, :, SL : SL + 1, :] = done.reshape(SP, 1, LANES)

    column_copies = []
    for i, (away, offset) in enumerate(offsets_of(2)):
        there = chip if away == 0 else 1 - chip
        other = other_of(offset)
        column_copies.append(
            pltpu.make_async_remote_copy(
                src_ref=column_out.at[there, other],
                dst_ref=column.at[chip, space],
                send_sem=a2a_send.at[i],
                recv_sem=a2a_recv.at[i],
                device_id=(on_chip[away], other),
                device_id_type=MESH,
            )
        )
    for copy in column_copies:
        copy.start()
    column[chip, space] = column_out[chip, space]
    for copy in column_copies:
        copy.wait_recv()
    both = column[0] + column[1]
    field_lanes = lax.broadcasted_iota(jnp.int32, (SP, 1, LANES), 2) // 64 == core
    edge = both[:, SL : SL + 1, :]
    lower = jnp.where(field_lanes, edge, 0.0)
    upper = jnp.where(field_lanes, pltpu.roll(edge.reshape(SP, LANES), 64, 1).reshape(SP, 1, LANES), 0.0)
    at_start = lower + jnp.concatenate([upper[SP - 1 :], upper[: SP - 1]], axis=0)
    at_end = upper + jnp.concatenate([lower[1:], lower[:1]], axis=0)
    place = lax.broadcasted_iota(jnp.int32, (SP, SL, LANES), 1)
    cells = both[:, 0:SL, :]
    cells = cells + jnp.where(place == 0, at_start, 0.0) + jnp.where(place == SL - 1, at_end, 0.0)

    spectral = table_times(tabs[0], cells.reshape(NX, LANES)) * spectrum[...]
    back_out[...] = table_times(tabs[0], spectral).reshape(SP, SL, LANES)

    back_copies = []
    for i, (_, offset) in enumerate(offsets_of(1)):
        other = other_of(offset)
        back_copies.append(
            pltpu.make_async_remote_copy(
                src_ref=back_out.at[other],
                dst_ref=back.at[space],
                send_sem=b2a_send.at[i],
                recv_sem=b2a_recv.at[i],
                device_id=(scen, other),
                device_id_type=MESH,
            )
        )
    for copy in back_copies:
        copy.start()
    back[space] = back_out[space]
    for copy in back_copies:
        copy.wait_recv()

    block_out[...] = table_times(tabs[2], back[...].reshape(256, LANES)).reshape(4, 64, LANES)
    block_copies = []
    for i in range(1, 4):
        other = lax.rem(scen + i, 4)
        block_copies.append(
            pltpu.make_async_remote_copy(
                src_ref=block_out.at[other],
                dst_ref=block.at[scen],
                send_sem=blk_send.at[i],
                recv_sem=blk_recv.at[i],
                device_id=(other, space),
                device_id_type=MESH,
            )
        )
    for copy in block_copies:
        copy.start()
    block[scen] = block_out[scen]
    for copy in cond_halo() + (part_copy, rim_copy):
        copy.wait_send()
    for copy in column_copies + back_copies:
        copy.wait_send()
    for s in range(NSC):
        for copy in adj_halo(s) + change_halo(s) + conc_halo(s):
            copy.wait_send()
    for copy in block_copies:
        copy.wait()

    out[...] = block[...]


def along_y(block, tabs, out):
    first = lax.broadcasted_iota(jnp.int32, (64, LANES), 1) < 64
    cond_f = [jnp.where(first, block[i], block[i + 1]) for i in (0, 2)]
    rate_f = [pltpu.roll(jnp.where(first, block[i + 1], block[i]), 64, 1) for i in (0, 2)]
    for which, halves in enumerate((cond_f, rate_f)):
        whole = jnp.concatenate(halves, axis=1)
        out[which] = times_table(whole, tabs).reshape(SL, 8, NY)


def body(states, terminal, log_cond, log_rate, well_cell, sample_step, well_misfit):
    hbm = pl.BlockSpec(memory_space=pltpu.HBM)
    smem = pl.BlockSpec(memory_space=pltpu.SMEM)
    vmem = pl.BlockSpec(memory_space=pltpu.VMEM)
    dma = pltpu.SemaphoreType.DMA
    slab = (SL, NZ, NY)
    scratch = [
        pltpu.VMEM((3, NSC, 3, SL + 2, NZ, NY), bf16),
        pltpu.VMEM((NSC, 3, SL + 2, NZ, NY), bf16),
        pltpu.VMEM((NSC, 3, SL + 2, NZ, NY), f32),
        pltpu.VMEM((NSC, 3, SL + 2, NZ, NY), f32),
        pltpu.VMEM((SL + 2, NZ, NY), f32),
        pltpu.VMEM(slab, f32),
        pltpu.VMEM((3, SL + 1, NZ, NY), f32),
        pltpu.VMEM((3,) + slab, f32),
        pltpu.VMEM((3,) + slab, f32),
        pltpu.VMEM((SL + 1, NZ, NY), f32),
        pltpu.VMEM(slab, f32),
        pltpu.VMEM(slab, f32),
        pltpu.VMEM(slab, f32),
        pltpu.VMEM((2, NSC, 3, NZ, NY), bf16),
        pltpu.VMEM((2, NSC, 3, NZ, NY), bf16),
        pltpu.VMEM((NSC, SL + 2, NZ, 32), bf16),
        pltpu.VMEM((3, NSC, 3, 32, NY), bf16),
        pltpu.VMEM((4, 2, 256, 256), bf16),
        pltpu.VMEM((NX, LANES), f32),
        pltpu.VMEM((2,) + slab, f32),
        pltpu.VMEM((2, 2, 256, LANES), f32),
        pltpu.VMEM((2, 256, LANES), f32),
        pltpu.VMEM((2, 2, NZ, LANES), f32),
        pltpu.VMEM((2, NZ, LANES), f32),
        pltpu.VMEM((2, SP, SL + 1, LANES), f32),
        pltpu.VMEM((2, SP, SL + 1, LANES), f32),
        pltpu.VMEM((SP, SL, LANES), f32),
        pltpu.VMEM((SP, SL, LANES), f32),
        pltpu.VMEM((4, 64, LANES), f32),
        pltpu.VMEM((4, 64, LANES), f32),
        dma((7,)),
        dma((26,)),
        dma((26,)),
        dma((2,)),
        dma((2,)),
        dma((2 * SP - 1,)),
        dma((2 * SP - 1,)),
        dma((SP - 1,)),
        dma((SP - 1,)),
        dma((4,)),
        dma((4,)),
    ]
    blocks = pl.pallas_call(
        kernel,
        out_shape=jax.ShapeDtypeStruct((4, 64, LANES), f32),
        in_specs=[hbm, hbm, hbm, hbm, smem, smem, smem, hbm],
        out_specs=vmem,
        scratch_shapes=scratch,
        compiler_params=pltpu.CompilerParams(
            collective_id=0, has_side_effects=True, vmem_limit_bytes=40 * 1024 * 1024
        ),
    )(
        *[
            pltpu.with_memory_space_constraint(value, pltpu.HBM)
            for value in (states, terminal, log_cond, log_rate)
        ],
        *[
            pltpu.with_memory_space_constraint(value, pltpu.HBM)
            for value in (well_cell, sample_step, jnp.transpose(well_misfit, (2, 0, 1)))
        ],
        pltpu.with_memory_space_constraint(jnp.asarray(tables()), pltpu.HBM),
    )
    line = jnp.asarray(two_parts(cas(np.arange(256), np.arange(256), 256)))
    return pl.pallas_call(
        along_y,
        out_shape=jax.ShapeDtypeStruct((2, SL, 8, NY), f32),
        in_specs=[vmem, vmem],
        out_specs=vmem,
        compiler_params=pltpu.CompilerParams(vmem_limit_bytes=8 * 1024 * 1024),
    )(blocks, line)


def solution(mesh):
    in_specs = (
        P(None, "scen", None, "space", None, None),
        P("scen", None, "space", None, None),
        P("space", None, None),
        P("space", None, None),
        P("scen", None),
        P("scen", None),
        P("scen", None, None),
    )
    out_specs = P(None, "space", "scen", None)
    return jax.shard_map(body, mesh=mesh, in_specs=in_specs, out_specs=out_specs, check_vma=False)
```

```python
import functools
import math

import jax
import jax.numpy as jnp
import numpy as np
from jax import lax
from jax.experimental import pallas as pl
from jax.experimental.pallas import tpu as pltpu
from jax.sharding import PartitionSpec as P

time_step = 0.05
diffusion = (1.0, 0.8, 0.1)
donor_half = 0.5
acceptor_half = 0.3
acceptor_yield = 0.5
biomass_yield = 0.4
lengths = (40.0, 24.0)
f32 = jnp.float32
bf16 = jnp.bfloat16
MESH = pl.DeviceIdType.MESH

SL = 8
NZ = 32
NY = 256
NSC = 4
NW = 8
SP = 32
NX = SL * SP
LANES = 128


def cas(rows, cols, count):
    angle = 2.0 * np.pi * (np.outer(rows, cols) % count) / count
    return np.cos(angle) + np.sin(angle)


def two_parts(table):
    high = table.astype(np.float32).astype(bf16)
    low = (table - high.astype(np.float64)).astype(np.float32).astype(bf16)
    return np.stack([high, low])


def tables():
    count = np.arange(256)
    line = cas(count, count, 256)
    small = cas(np.arange(NZ), np.arange(NZ), NZ)
    ahead = np.zeros((NZ, SL, SL, NZ))
    back = np.zeros((4, SL, 8, NZ, SL))
    for x in range(SL):
        ahead[:, x, x, :] = small
        back[:, x, :, :, x] = small.reshape(4, 8, NZ)
    corner = np.zeros((256, 256))
    corner[:NZ, :NZ] = small
    turned = [line, ahead.reshape(256, 256), back.reshape(256, 256), corner]
    next_y = np.eye(NY, k=-1) - np.eye(NY)
    next_y[:, -1] = 0.0
    next_z = np.eye(NZ, k=1) - np.eye(NZ)
    next_z[-1] = 0.0
    three = np.zeros((256, 256))
    three[: 3 * NZ, : 3 * NZ] = np.kron(np.eye(3), next_z)
    steps = np.stack([next_y, three]).astype(np.float32).astype(bf16)
    return np.stack([two_parts(table) for table in turned] + [steps])


def offsets_of(chips):
    found = []
    for away in range(chips):
        for i in range(SP):
            x, z, y = i // 8, i // 2 % 4, i % 2
            hops = min(x, 4 - x) + min(z, 4 - z) + (1 if away else 2 * y)
            if hops:
                found.append((-hops, i, away, (x, z, y)))
    return [(away, offset) for _, _, away, offset in sorted(found)]


def split2(value):
    high = value.astype(bf16)
    low = (value - high.astype(f32)).astype(bf16)
    return high, low


def mm(a, b):
    return jnp.dot(a, b, preferred_element_type=f32)


def table_times(table, data):
    high, low = split2(data)
    return mm(table[0], high) + mm(table[0], low) + mm(table[1], high)


def times_table(data, table):
    high, low = split2(data)
    return mm(high, table[0]) + mm(low, table[0]) + mm(high, table[1])


def kernel(
    states,
    terminal,
    log_cond,
    log_rate,
    cell_hbm,
    sample_hbm,
    misfit_hbm,
    tabs_hbm,
    out,
    conc,
    adj3,
    adj2,
    adj1,
    cond,
    rate,
    weight_x,
    weight_z,
    weight_y,
    total_x,
    total_z,
    total_y,
    total_r,
    change,
    change_in,
    well_cell,
    sample_step,
    well_misfit,
    hot,
    inject,
    flux,
    tabs,
    spectrum,
    grad,
    part,
    part_in,
    rim,
    rim_in,
    column_out,
    column,
    back_out,
    back,
    block_out,
    block,
    local_sem,
    halo_send,
    halo_recv,
    sum_send,
    sum_recv,
    a2a_send,
    a2a_recv,
    b2a_send,
    b2a_recv,
    blk_send,
    blk_recv,
):
    scen = lax.axis_index("scen")
    space = lax.axis_index("space")
    chip = scen // 2
    core = lax.rem(scen, 2)
    left = lax.rem(space + SP - 1, SP)
    right = lax.rem(space + 1, SP)

    local = [
        pltpu.make_async_copy(terminal, adj3.at[:, :, 1 : 1 + SL], local_sem.at[0]),
        pltpu.make_async_copy(log_cond, cond.at[1 : 1 + SL], local_sem.at[1]),
        pltpu.make_async_copy(log_rate, rate, local_sem.at[2]),
        pltpu.make_async_copy(states.at[2], conc.at[2, :, :, 1 : 1 + SL], local_sem.at[3]),
        pltpu.make_async_copy(states.at[1], conc.at[1, :, :, 1 : 1 + SL], local_sem.at[4]),
        pltpu.make_async_copy(states.at[0], conc.at[0, :, :, 1 : 1 + SL], local_sem.at[5]),
        pltpu.make_async_copy(tabs_hbm, tabs, local_sem.at[6]),
        pltpu.make_async_copy(cell_hbm, well_cell, local_sem.at[7]),
        pltpu.make_async_copy(sample_hbm, sample_step, local_sem.at[8]),
        pltpu.make_async_copy(misfit_hbm, well_misfit, local_sem.at[9]),
    ]
    for i in (1, 2, 7, 8, 9, 0, 3, 6, 4, 5):
        local[i].start()

    part_x = [lax.rem(space // 8 + i, 4) * 8 for i in range(4)]
    part_z = [lax.rem(space // 2 + i, 4) * 2 for i in range(4)]
    part_y = [lax.rem(space + i, 2) for i in range(2)]
    on_chip = [chip * 2 + core, (1 - chip) * 2 + core]

    def other_of(offset):
        return part_x[offset[0]] + part_z[offset[1]] + part_y[offset[2]]

    barrier = pltpu.get_barrier_semaphore()

    def signal(to_scen, to_space):
        pl.semaphore_signal(
            barrier, inc=1, device_id=(to_scen, to_space), device_id_type=MESH
        )

    for away, offset in offsets_of(2):
        signal(on_chip[away], other_of(offset))
    signal(chip * 2 + 1 - core, space)
    signal((1 - chip) * 2 + 1 - core, space)
    pl.semaphore_wait(barrier, 2 * (SP - 1) + 3)

    def to_side(i, source, target, side):
        return pltpu.make_async_remote_copy(
            src_ref=source,
            dst_ref=target,
            send_sem=halo_send.at[i],
            recv_sem=halo_recv.at[i],
            device_id=(scen, side),
            device_id_type=MESH,
        )

    def cond_halo():
        return (
            to_side(0, log_cond.at[SL - 1], cond.at[0], right),
            to_side(1, log_cond.at[0], cond.at[SL + 1], left),
        )

    def adj_halo(s):
        return (
            to_side(2 + s, terminal.at[s, :, SL - 1], adj3.at[s, :, 0], right),
            to_side(6 + s, terminal.at[s, :, 0], adj3.at[s, :, SL + 1], left),
        )

    def change_halo(s):
        return (
            to_side(10 + s, change.at[1, s], change_in.at[0, s], right),
            to_side(14 + s, change.at[0, s], change_in.at[1, s], left),
        )

    def conc_halo(s):
        return (
            to_side(18 + s, states.at[0, s, :, SL - 1], conc.at[0, s, :, 0], right),
            to_side(22 + s, states.at[0, s, :, 0], conc.at[0, s, :, SL + 1], left),
        )

    for copy in cond_halo():
        copy.start()
    for s in range(NSC):
        for copy in adj_halo(s):
            copy.start()

    nothing = jnp.zeros((NZ, NY), f32)
    for s in range(NSC):
        for sp in range(3):
            for side in (0, SL + 1):
                conc[1, s, sp, side] = nothing.astype(bf16)
                conc[2, s, sp, side] = nothing.astype(bf16)
                adj1[s, sp, side] = nothing

    def clear(x, carry):
        total_x[x] = nothing
        total_z[x] = nothing
        total_y[x] = nothing
        total_r[x] = nothing
        return carry

    lax.fori_loop(0, SL, clear, 0)
    total_x[SL] = nothing

    local[1].wait()
    local[2].wait()
    z_index = lax.broadcasted_iota(jnp.int32, (NZ, NY), 0)
    y_index = lax.broadcasted_iota(jnp.int32, (NZ, NY), 1)

    def own_weights(x, carry):
        here = jnp.exp(cond[x])
        cond[x] = here
        rate[x - 1] = jnp.exp(rate[x - 1])
        above = jnp.sqrt(here * pltpu.roll(here, NZ - 1, 0))
        above = jnp.where(z_index == NZ - 1, 0.0, above)
        beside = jnp.sqrt(here * pltpu.roll(here, NY - 1, 1))
        beside = jnp.where(y_index == NY - 1, 0.0, beside)
        for sp in range(3):
            weight_z[sp, x - 1] = (time_step * diffusion[sp]) * above
            weight_y[sp, x - 1] = (time_step * diffusion[sp]) * beside
        return carry

    lax.fori_loop(1, SL + 1, own_weights, 0)

    def inner_weights(x, carry):
        between = jnp.sqrt(cond[x] * cond[x + 1])
        for sp in range(3):
            weight_x[sp, x] = (time_step * diffusion[sp]) * between
        return carry

    lax.fori_loop(1, SL, inner_weights, 0)

    for i in (7, 8, 9):
        local[i].wait()
    lane = lax.broadcasted_iota(jnp.int32, (1, 32), 1)
    row_at = lax.broadcasted_iota(jnp.int32, (NZ, 32), 0)
    well_row = lax.broadcasted_iota(jnp.int32, (NW, NY), 0)
    well_col = lax.broadcasted_iota(jnp.int32, (NW, NY), 1)

    def wells(s, carry):
        row_of = jnp.full((1, 32), -1, jnp.int32)
        col_of = jnp.zeros((NW, NY), jnp.int32)
        step_of = jnp.zeros((NW, NY), jnp.int32)
        amounts = [jnp.zeros((NW, NY), f32)] * 3
        for w in range(NW):
            cell = well_cell[s, w]
            row = ((cell - space * (SL * NZ * NY)) >> 8) + NZ
            row_of = jnp.where(lane % NW == w, row, row_of)
            col_of = jnp.where(well_row == w, cell & 255, col_of)
            step_of = jnp.where(well_row == w, sample_step[s, w], step_of)
            amounts = [
                jnp.where(well_row == w, well_misfit[sp, s, w], amounts[sp]) for sp in range(3)
            ]
        row_of = jnp.where(lane < 3 * NW, row_of, -1)
        for x in range(SL + 2):
            hot[s, x] = jnp.where(row_at + x * NZ == row_of, 1.0, 0.0).astype(bf16)
        here = well_col == col_of
        for n in (1, 2):
            chosen = here & (step_of == n)
            for sp in range(3):
                value = jnp.where(chosen, amounts[sp], 0.0)
                high = value.astype(bf16).astype(f32)
                rest = value - high
                middle = rest.astype(bf16).astype(f32)
                low = rest - middle
                inject[n, s, :, sp * NY : (sp + 1) * NY] = jnp.concatenate(
                    [high, middle, low, jnp.zeros((NW, NY), f32)], axis=0
                ).astype(bf16)
        return carry

    lax.fori_loop(0, NSC, wells, 0)

    def x_face(n, adj, s, x, keep=False):
        total = total_x[x]
        for sp in range(3):
            step_a = adj[s, sp, x + 1].astype(f32) - adj[s, sp, x].astype(f32)
            step_c = conc[n, s, sp, x + 1].astype(f32) - conc[n, s, sp, x].astype(f32)
            through = weight_x[sp, x] * step_a
            total = total + step_c * through
            if keep:
                flux[s, sp, x] = through
        total_x[x] = total

    def injected(n, s, x):
        added = mm(hot[s, x], inject[n, s])
        return [added[:, sp * NY : (sp + 1) * NY] for sp in range(3)]

    def layer(n, adj, new, s, x, side=None, face=True):
        own = x - 1
        three = conc[n, s, :, x].reshape(3 * NZ, NY)
        steps_y = mm(three, tabs[4, 0])
        steps_z = mm(tabs[4, 1, 0 : 3 * NZ, 0 : 3 * NZ], three)
        conc_here = [conc[n, s, sp, x].astype(f32) for sp in range(3)]
        adj_here = [adj[s, sp, x].astype(f32) for sp in range(3)]
        sum_z = total_z[own]
        sum_y = total_y[own]
        if face:
            sum_x = total_x[x]
        spread = []
        for sp in range(3):
            a = adj_here[sp]
            rows = slice(sp * NZ, (sp + 1) * NZ)
            flux_z = weight_z[sp, own] * (pltpu.roll(a, NZ - 1, 0) - a)
            flux_y = weight_y[sp, own] * (pltpu.roll(a, NY - 1, 1) - a)
            sum_z = sum_z + steps_z[rows] * flux_z
            sum_y = sum_y + steps_y[rows] * flux_y
            if face:
                flux_x = weight_x[sp, x] * (adj[s, sp, x + 1].astype(f32) - a)
                step_c = conc[n, s, sp, x + 1].astype(f32) - conc_here[sp]
                sum_x = sum_x + step_c * flux_x
                if new is not None:
                    flux[s, sp, x] = flux_x
            elif new is not None:
                flux_x = flux[s, sp, x]
            if new is not None:
                spread.append(
                    (flux_x - flux[s, sp, x - 1])
                    + (flux_z - pltpu.roll(flux_z, 1, 0))
                    + (flux_y - pltpu.roll(flux_y, 1, 1))
                )
        if face:
            total_x[x] = sum_x
        total_z[own] = sum_z
        total_y[own] = sum_y
        donor, acceptor, biomass = conc_here
        donor_inv = 1.0 / (donor_half + donor)
        accept_inv = 1.0 / (acceptor_half + acceptor)
        donor_mono = donor * donor_inv
        accept_mono = acceptor * accept_inv
        both = donor_mono * accept_mono
        stoich = -adj_here[0] - acceptor_yield * adj_here[1] + biomass_yield * adj_here[2]
        scaled = (time_step * stoich) * rate[own]
        growth = scaled * biomass
        total_r[own] = total_r[own] + growth * both
        if new is None:
            return
        spread[0] = spread[0] + (growth * accept_mono) * (donor_half * (donor_inv * donor_inv))
        spread[1] = spread[1] + (growth * donor_mono) * (acceptor_half * (accept_inv * accept_inv))
        spread[2] = spread[2] + scaled * both
        added = injected(n, s, x)
        for sp in range(3):
            if side is not None:
                change[side, s, sp] = spread[sp].astype(bf16)
            new[s, sp, x] = adj_here[sp] + spread[sp] + added[sp]

    def layers(n, adj, new, s, first, last):
        def two(i, carry):
            layer(n, adj, new, s, first + 2 * i)
            layer(n, adj, new, s, first + 2 * i + 1)
            return carry

        lax.fori_loop(0, (last - first) // 2, two, 0)

    def inner(n, adj, new, s):
        x_face(n, adj, s, 1, True)
        layers(n, adj, new, s, 2, SL)

    def outer(n, adj, new, s, sides=(None, None)):
        x_face(n, adj, s, 0, True)
        layer(n, adj, new, s, 1, sides[0], face=False)
        layer(n, adj, new, s, SL, sides[1])

    local[0].wait()
    local[3].wait()
    local[6].wait()

    def inner_two(s, carry):
        inner(2, adj3, adj2, s)
        return carry

    lax.fori_loop(0, NSC, inner_two, 0)
    for copy in cond_halo():
        copy.wait_recv()
    for x, beyond, wall in ((0, 0, space == 0), (SL, SL + 1, space == SP - 1)):
        between = jnp.sqrt(jnp.exp(cond[beyond]) * cond[2 * x + 1 - beyond])
        between = jnp.where(wall, 0.0, between)
        for sp in range(3):
            weight_x[sp, x] = (time_step * diffusion[sp]) * between
    local[4].wait()

    def two_and_one(s, carry):
        for copy in adj_halo(s):
            copy.wait_recv()
        outer(2, adj3, adj2, s, (0, 1))
        for copy in change_halo(s):
            copy.start()
        inner(1, adj2, adj1, s)
        return carry

    lax.fori_loop(0, NSC, two_and_one, 0)
    row = lax.broadcasted_iota(jnp.int32, (NX, LANES), 0)
    col = lax.broadcasted_iota(jnp.int32, (NX, LANES), 1)
    wave_x = jnp.minimum(row, NX - row).astype(f32) * (2.0 * math.pi / NX)
    freq_y = scen * 64 + col % 64
    wave_y = jnp.minimum(freq_y, NY - freq_y).astype(f32) * (2.0 * math.pi / NY)
    freq_z = jnp.full((1, LANES), space, jnp.int32)
    wave_z = jnp.minimum(freq_z, NZ - freq_z).astype(f32) * (2.0 * math.pi / NZ)
    field = (col // 64 + scen) % 2
    length = jnp.where(field == 0, lengths[0], lengths[1])
    square = wave_x * wave_x + wave_z * wave_z + wave_y * wave_y
    spectrum[...] = (length / jnp.sqrt(1.0 + (length * length) * square)) * (1.0 / (NX * NZ * NY))
    local[5].wait()

    def one_and_none(s, carry):
        for copy in change_halo(s):
            copy.wait_recv()
        for side, x in ((0, 0), (1, SL + 1)):
            added = injected(2, s, x)
            for sp in range(3):
                adj2[s, sp, x] = (
                    adj3[s, sp, x].astype(f32) + change_in[side, s, sp].astype(f32) + added[sp]
                )
        for copy in conc_halo(s):
            copy.start()
        outer(1, adj2, adj1, s)
        layers(0, adj1, None, s, 1, SL - 1)
        layer(0, adj1, None, s, SL - 1)
        layer(0, adj1, None, s, SL, face=False)
        return carry

    lax.fori_loop(0, NSC, one_and_none, 0)

    def gradients(x, carry):
        along_z = total_z[x]
        along_y = total_y[x]
        total = along_z + pltpu.roll(along_z, 1, 0) + along_y + pltpu.roll(along_y, 1, 1)
        before = jnp.where(x == 0, 0.0, total_x[x])
        after = jnp.where(x == SL - 1, 0.0, total_x[x + 1])
        grad[0, x] = -0.5 * (total + before + after)
        grad[1, x] = total_r[x]
        return carry

    lax.fori_loop(0, SL, gradients, 0)

    first = lax.broadcasted_iota(jnp.int32, (256, LANES), 1) < 64
    cond_y = times_table(grad[0].reshape(256, NY), tabs[0])
    rate_y = times_table(grad[1].reshape(256, NY), tabs[0])
    for i in range(2):
        lanes = slice(i * LANES, (i + 1) * LANES)
        a = cond_y[:, lanes]
        b = pltpu.roll(rate_y[:, lanes], 64, 1)
        part[0, i] = jnp.where(first, a, b)
        part[1, i] = jnp.where(first, b, a)

    def to_mate(i, source, target):
        return pltpu.make_async_remote_copy(
            src_ref=source,
            dst_ref=target,
            send_sem=sum_send.at[i],
            recv_sem=sum_recv.at[i],
            device_id=(chip * 2 + 1 - core, space),
            device_id_type=MESH,
        )

    part_copy = to_mate(0, part.at[1 - core], part_in)
    part_copy.start()
    part_copy.wait_recv()
    for i in range(2):
        done = table_times(tabs[1], part[core, i] + part_in[i])
        column_out[i, :, 0:SL, :] = done.reshape(SP, SL, LANES)

    def none_faces(s, carry):
        for copy in conc_halo(s):
            copy.wait_recv()
        x_face(0, adj1, s, 0)
        x_face(0, adj1, s, SL)
        return carry

    lax.fori_loop(0, NSC, none_faces, 0)
    faces = jnp.concatenate([total_x[0], total_x[SL]], axis=0) * -0.5
    faces_y = times_table(faces, tabs[0])
    first_rim = lax.broadcasted_iota(jnp.int32, (NZ, LANES), 1) < 64
    for i in range(2):
        lanes = slice(i * LANES, (i + 1) * LANES)
        a = faces_y[0:NZ, lanes]
        b = pltpu.roll(faces_y[NZ : 2 * NZ, lanes], 64, 1)
        rim[0, i] = jnp.where(first_rim, a, b)
        rim[1, i] = jnp.where(first_rim, b, a)
    rim_copy = to_mate(1, rim.at[1 - core], rim_in)
    rim_copy.start()
    rim_copy.wait_recv()
    for i in range(2):
        done = table_times(tabs[3, :, 0:NZ, 0:NZ], rim[core, i] + rim_in[i])
        column_out[i, :, SL : SL + 1, :] = done.reshape(SP, 1, LANES)

    column_copies = []
    for i, (away, offset) in enumerate(offsets_of(2)):
        there = chip if away == 0 else 1 - chip
        other = other_of(offset)
        column_copies.append(
            pltpu.make_async_remote_copy(
                src_ref=column_out.at[there, other],
                dst_ref=column.at[chip, space],
                send_sem=a2a_send.at[i],
                recv_sem=a2a_recv.at[i],
                device_id=(on_chip[away], other),
                device_id_type=MESH,
            )
        )
    for copy in column_copies:
        copy.start()
    column[chip, space] = column_out[chip, space]
    for copy in column_copies:
        copy.wait_recv()
    both = column[0] + column[1]
    field_lanes = lax.broadcasted_iota(jnp.int32, (SP, 1, LANES), 2) // 64 == core
    edge = both[:, SL : SL + 1, :]
    lower = jnp.where(field_lanes, edge, 0.0)
    upper = jnp.where(field_lanes, pltpu.roll(edge.reshape(SP, LANES), 64, 1).reshape(SP, 1, LANES), 0.0)
    at_start = lower + jnp.concatenate([upper[SP - 1 :], upper[: SP - 1]], axis=0)
    at_end = upper + jnp.concatenate([lower[1:], lower[:1]], axis=0)
    place = lax.broadcasted_iota(jnp.int32, (SP, SL, LANES), 1)
    cells = both[:, 0:SL, :]
    cells = cells + jnp.where(place == 0, at_start, 0.0) + jnp.where(place == SL - 1, at_end, 0.0)

    spectral = table_times(tabs[0], cells.reshape(NX, LANES)) * spectrum[...]
    back_out[...] = table_times(tabs[0], spectral).reshape(SP, SL, LANES)

    back_copies = []
    for i, (_, offset) in enumerate(offsets_of(1)):
        other = other_of(offset)
        back_copies.append(
            pltpu.make_async_remote_copy(
                src_ref=back_out.at[other],
                dst_ref=back.at[space],
                send_sem=b2a_send.at[i],
                recv_sem=b2a_recv.at[i],
                device_id=(scen, other),
                device_id_type=MESH,
            )
        )
    for copy in back_copies:
        copy.start()
    back[space] = back_out[space]
    for copy in back_copies:
        copy.wait_recv()

    back_high, back_low = split2(back[...].reshape(256, LANES))

    def z_blocks(which):
        rows = pl.ds(pl.multiple_of(which * 128, 128), 128)
        high, low = tabs[2, 0, rows, :], tabs[2, 1, rows, :]
        done = mm(high, back_high) + mm(high, back_low) + mm(low, back_high)
        return done.reshape(2, 64, LANES)

    def block_copy(i, other):
        return pltpu.make_async_remote_copy(
            src_ref=block_out.at[other],
            dst_ref=block.at[scen],
            send_sem=blk_send.at[i],
            recv_sem=blk_recv.at[i],
            device_id=(other, space),
            device_id_type=MESH,
        )

    block_copies = [
        block_copy(1, (1 - chip) * 2 + core),
        block_copy(2, (1 - chip) * 2 + 1 - core),
        block_copy(3, chip * 2 + 1 - core),
    ]
    block_out[pl.ds((1 - chip) * 2, 2)] = z_blocks(1 - chip)
    block_copies[0].start()
    block_copies[1].start()
    block_out[pl.ds(chip * 2, 2)] = z_blocks(chip)
    block_copies[2].start()
    block[scen] = block_out[scen]
    for copy in cond_halo() + (part_copy, rim_copy):
        copy.wait_send()
    for copy in column_copies + back_copies:
        copy.wait_send()
    for s in range(NSC):
        for copy in adj_halo(s) + change_halo(s) + conc_halo(s):
            copy.wait_send()
    for copy in block_copies:
        copy.wait()

    out[...] = block[...]


def along_y(block, tabs, out):
    first = lax.broadcasted_iota(jnp.int32, (64, LANES), 1) < 64
    cond_f = [jnp.where(first, block[i], block[i + 1]) for i in (0, 2)]
    rate_f = [pltpu.roll(jnp.where(first, block[i + 1], block[i]), 64, 1) for i in (0, 2)]
    for which, halves in enumerate((cond_f, rate_f)):
        whole = jnp.concatenate(halves, axis=1)
        out[which] = times_table(whole, tabs).reshape(SL, 8, NY)


def body(states, terminal, log_cond, log_rate, well_cell, sample_step, well_misfit):
    hbm = pl.BlockSpec(memory_space=pltpu.HBM)
    vmem = pl.BlockSpec(memory_space=pltpu.VMEM)
    dma = pltpu.SemaphoreType.DMA
    slab = (SL, NZ, NY)
    scratch = [
        pltpu.VMEM((3, NSC, 3, SL + 2, NZ, NY), bf16),
        pltpu.VMEM((NSC, 3, SL + 2, NZ, NY), bf16),
        pltpu.VMEM((NSC, 3, SL + 2, NZ, NY), f32),
        pltpu.VMEM((NSC, 3, SL + 2, NZ, NY), f32),
        pltpu.VMEM((SL + 2, NZ, NY), f32),
        pltpu.VMEM(slab, f32),
        pltpu.VMEM((3, SL + 1, NZ, NY), f32),
        pltpu.VMEM((3,) + slab, f32),
        pltpu.VMEM((3,) + slab, f32),
        pltpu.VMEM((SL + 1, NZ, NY), f32),
        pltpu.VMEM(slab, f32),
        pltpu.VMEM(slab, f32),
        pltpu.VMEM(slab, f32),
        pltpu.VMEM((2, NSC, 3, NZ, NY), bf16),
        pltpu.VMEM((2, NSC, 3, NZ, NY), bf16),
        pltpu.SMEM((NSC, NW), jnp.int32),
        pltpu.SMEM((NSC, NW), jnp.int32),
        pltpu.SMEM((3, NSC, NW), f32),
        pltpu.VMEM((NSC, SL + 2, NZ, 32), bf16),
        pltpu.VMEM((3, NSC, 32, 3 * NY), bf16),
        pltpu.VMEM((NSC, 3, SL + 1, NZ, NY), f32),
        pltpu.VMEM((5, 2, 256, 256), bf16),
        pltpu.VMEM((NX, LANES), f32),
        pltpu.VMEM((2,) + slab, f32),
        pltpu.VMEM((2, 2, 256, LANES), f32),
        pltpu.VMEM((2, 256, LANES), f32),
        pltpu.VMEM((2, 2, NZ, LANES), f32),
        pltpu.VMEM((2, NZ, LANES), f32),
        pltpu.VMEM((2, SP, SL + 1, LANES), f32),
        pltpu.VMEM((2, SP, SL + 1, LANES), f32),
        pltpu.VMEM((SP, SL, LANES), f32),
        pltpu.VMEM((SP, SL, LANES), f32),
        pltpu.VMEM((4, 64, LANES), f32),
        pltpu.VMEM((4, 64, LANES), f32),
        dma((10,)),
        dma((26,)),
        dma((26,)),
        dma((2,)),
        dma((2,)),
        dma((2 * SP - 1,)),
        dma((2 * SP - 1,)),
        dma((SP - 1,)),
        dma((SP - 1,)),
        dma((4,)),
        dma((4,)),
    ]
    blocks = pl.pallas_call(
        kernel,
        out_shape=jax.ShapeDtypeStruct((4, 64, LANES), f32),
        in_specs=[hbm] * 8,
        out_specs=vmem,
        scratch_shapes=scratch,
        compiler_params=pltpu.CompilerParams(
            collective_id=0, has_side_effects=True, vmem_limit_bytes=40 * 1024 * 1024
        ),
    )(
        *[
            pltpu.with_memory_space_constraint(value, pltpu.HBM)
            for value in (states, terminal, log_cond, log_rate)
        ],
        *[
            pltpu.with_memory_space_constraint(value, pltpu.HBM)
            for value in (well_cell, sample_step, jnp.transpose(well_misfit, (2, 0, 1)))
        ],
        pltpu.with_memory_space_constraint(jnp.asarray(tables()), pltpu.HBM),
    )
    line = jnp.asarray(two_parts(cas(np.arange(256), np.arange(256), 256)))
    return pl.pallas_call(
        along_y,
        out_shape=jax.ShapeDtypeStruct((2, SL, 8, NY), f32),
        in_specs=[vmem, vmem],
        out_specs=vmem,
        compiler_params=pltpu.CompilerParams(vmem_limit_bytes=8 * 1024 * 1024),
    )(blocks, line)


def solution(mesh):
    in_specs = (
        P(None, "scen", None, "space", None, None),
        P("scen", None, "space", None, None),
        P("space", None, None),
        P("space", None, None),
        P("scen", None),
        P("scen", None),
        P("scen", None, None),
    )
    out_specs = P(None, "space", "scen", None)
    return jax.shard_map(body, mesh=mesh, in_specs=in_specs, out_specs=out_specs, check_vma=False)
```

```python
import functools
import math

import jax
import jax.numpy as jnp
import numpy as np
from jax import lax
from jax.experimental import pallas as pl
from jax.experimental.pallas import tpu as pltpu
from jax.sharding import PartitionSpec as P

time_step = 0.05
diffusion = (1.0, 0.8, 0.1)
donor_half = 0.5
acceptor_half = 0.3
acceptor_yield = 0.5
biomass_yield = 0.4
lengths = (40.0, 24.0)
f32 = jnp.float32
bf16 = jnp.bfloat16
MESH = pl.DeviceIdType.MESH

SL = 8
NZ = 32
NY = 256
NSC = 4
NW = 8
SP = 32
NX = SL * SP
LANES = 128


def cas(rows, cols, count):
    angle = 2.0 * np.pi * (np.outer(rows, cols) % count) / count
    return np.cos(angle) + np.sin(angle)


def two_parts(table):
    high = table.astype(np.float32).astype(bf16)
    low = (table - high.astype(np.float64)).astype(np.float32).astype(bf16)
    return np.stack([high, low])


def tables():
    count = np.arange(256)
    line = cas(count, count, 256)
    small = cas(np.arange(NZ), np.arange(NZ), NZ)
    ahead = np.zeros((NZ, SL, SL, NZ))
    back = np.zeros((4, SL, 8, NZ, SL))
    for x in range(SL):
        ahead[:, x, x, :] = small
        back[:, x, :, :, x] = small.reshape(4, 8, NZ)
    corner = np.zeros((256, 256))
    corner[:NZ, :NZ] = small
    turned = [line, ahead.reshape(256, 256), back.reshape(256, 256), corner]
    next_y = np.eye(NY, k=-1) - np.eye(NY)
    next_y[:, -1] = 0.0
    next_z = np.eye(NZ, k=1) - np.eye(NZ)
    next_z[-1] = 0.0
    three = np.zeros((256, 256))
    three[: 3 * NZ, : 3 * NZ] = np.kron(np.eye(3), next_z)
    steps = np.stack([next_y, three]).astype(np.float32).astype(bf16)
    return np.stack([two_parts(table) for table in turned] + [steps])


def offsets_of(chips):
    found = []
    for away in range(chips):
        for i in range(SP):
            x, z, y = i // 8, i // 2 % 4, i % 2
            hops = min(x, 4 - x) + min(z, 4 - z) + (1 if away else 2 * y)
            if hops:
                found.append((-hops, i, away, (x, z, y)))
    return [(away, offset) for _, _, away, offset in sorted(found)]


def split2(value):
    high = value.astype(bf16)
    low = (value - high.astype(f32)).astype(bf16)
    return high, low


def mm(a, b):
    return jnp.dot(a, b, preferred_element_type=f32)


def table_times(table, data):
    high, low = split2(data)
    width = data.shape[1]
    both = mm(table[0], jnp.concatenate([high, low], axis=1))
    return both[:, :width] + both[:, width:] + mm(table[1], high)


def times_table(data, table):
    high, low = split2(data)
    return mm(high, table[0]) + mm(low, table[0]) + mm(high, table[1])


def kernel(
    states,
    terminal,
    log_cond,
    log_rate,
    cell_hbm,
    sample_hbm,
    misfit_hbm,
    tabs_hbm,
    out,
    conc,
    adj3,
    adj2,
    adj1,
    cond,
    rate,
    weight_x,
    weight_z,
    weight_y,
    total_x,
    total_z,
    total_y,
    total_r,
    change,
    change_in,
    well_cell,
    sample_step,
    well_misfit,
    hot,
    inject,
    flux,
    tabs,
    spectrum,
    grad,
    part,
    part_in,
    rim,
    rim_in,
    column_out,
    column,
    back_out,
    back,
    block_out,
    block,
    local_sem,
    halo_send,
    halo_recv,
    sum_send,
    sum_recv,
    a2a_send,
    a2a_recv,
    b2a_send,
    b2a_recv,
    blk_send,
    blk_recv,
):
    scen = lax.axis_index("scen")
    space = lax.axis_index("space")
    chip = scen // 2
    core = lax.rem(scen, 2)
    left = lax.rem(space + SP - 1, SP)
    right = lax.rem(space + 1, SP)

    local = [
        pltpu.make_async_copy(terminal, adj3.at[:, :, 1 : 1 + SL], local_sem.at[0]),
        pltpu.make_async_copy(log_cond, cond.at[1 : 1 + SL], local_sem.at[1]),
        pltpu.make_async_copy(log_rate, rate, local_sem.at[2]),
        pltpu.make_async_copy(states.at[2], conc.at[2, :, :, 1 : 1 + SL], local_sem.at[3]),
        pltpu.make_async_copy(states.at[1], conc.at[1, :, :, 1 : 1 + SL], local_sem.at[4]),
        pltpu.make_async_copy(states.at[0], conc.at[0, :, :, 1 : 1 + SL], local_sem.at[5]),
        pltpu.make_async_copy(tabs_hbm, tabs, local_sem.at[6]),
        pltpu.make_async_copy(cell_hbm, well_cell, local_sem.at[7]),
        pltpu.make_async_copy(sample_hbm, sample_step, local_sem.at[8]),
        pltpu.make_async_copy(misfit_hbm, well_misfit, local_sem.at[9]),
    ]
    for i in (1, 2, 7, 8, 9, 0, 3, 6, 4, 5):
        local[i].start()

    part_x = [lax.rem(space // 8 + i, 4) * 8 for i in range(4)]
    part_z = [lax.rem(space // 2 + i, 4) * 2 for i in range(4)]
    part_y = [lax.rem(space + i, 2) for i in range(2)]
    on_chip = [chip * 2 + core, (1 - chip) * 2 + core]

    def other_of(offset):
        return part_x[offset[0]] + part_z[offset[1]] + part_y[offset[2]]

    barrier = pltpu.get_barrier_semaphore()

    def signal(to_scen, to_space):
        pl.semaphore_signal(
            barrier, inc=1, device_id=(to_scen, to_space), device_id_type=MESH
        )

    for away, offset in offsets_of(2):
        signal(on_chip[away], other_of(offset))
    signal(chip * 2 + 1 - core, space)
    signal((1 - chip) * 2 + 1 - core, space)
    pl.semaphore_wait(barrier, 2 * (SP - 1) + 3)

    def to_side(i, source, target, side):
        return pltpu.make_async_remote_copy(
            src_ref=source,
            dst_ref=target,
            send_sem=halo_send.at[i],
            recv_sem=halo_recv.at[i],
            device_id=(scen, side),
            device_id_type=MESH,
        )

    def cond_halo():
        return (
            to_side(0, log_cond.at[SL - 1], cond.at[0], right),
            to_side(1, log_cond.at[0], cond.at[SL + 1], left),
        )

    def adj_halo(s):
        return (
            to_side(2 + s, terminal.at[s, :, SL - 1], adj3.at[s, :, 0], right),
            to_side(6 + s, terminal.at[s, :, 0], adj3.at[s, :, SL + 1], left),
        )

    def change_halo(s):
        return (
            to_side(10 + s, change.at[1, s], change_in.at[0, s], right),
            to_side(14 + s, change.at[0, s], change_in.at[1, s], left),
        )

    def conc_halo(s):
        return (
            to_side(18 + s, states.at[0, s, :, SL - 1], conc.at[0, s, :, 0], right),
            to_side(22 + s, states.at[0, s, :, 0], conc.at[0, s, :, SL + 1], left),
        )

    for copy in cond_halo():
        copy.start()
    for s in range(NSC):
        for copy in adj_halo(s):
            copy.start()

    nothing = jnp.zeros((NZ, NY), f32)
    for s in range(NSC):
        for sp in range(3):
            for side in (0, SL + 1):
                conc[1, s, sp, side] = nothing.astype(bf16)
                conc[2, s, sp, side] = nothing.astype(bf16)
                adj1[s, sp, side] = nothing

    def clear(x, carry):
        total_x[x] = nothing
        total_z[x] = nothing
        total_y[x] = nothing
        total_r[x] = nothing
        return carry

    lax.fori_loop(0, SL, clear, 0)
    total_x[SL] = nothing

    local[1].wait()
    local[2].wait()
    z_index = lax.broadcasted_iota(jnp.int32, (NZ, NY), 0)
    y_index = lax.broadcasted_iota(jnp.int32, (NZ, NY), 1)

    def own_weights(x, carry):
        here = jnp.exp(cond[x])
        cond[x] = here
        rate[x - 1] = jnp.exp(rate[x - 1])
        above = jnp.sqrt(here * pltpu.roll(here, NZ - 1, 0))
        above = jnp.where(z_index == NZ - 1, 0.0, above)
        beside = jnp.sqrt(here * pltpu.roll(here, NY - 1, 1))
        beside = jnp.where(y_index == NY - 1, 0.0, beside)
        for sp in range(3):
            weight_z[sp, x - 1] = (time_step * diffusion[sp]) * above
            weight_y[sp, x - 1] = (time_step * diffusion[sp]) * beside
        return carry

    lax.fori_loop(1, SL + 1, own_weights, 0)

    def inner_weights(x, carry):
        between = jnp.sqrt(cond[x] * cond[x + 1])
        for sp in range(3):
            weight_x[sp, x] = (time_step * diffusion[sp]) * between
        return carry

    lax.fori_loop(1, SL, inner_weights, 0)

    for i in (7, 8, 9):
        local[i].wait()
    lane = lax.broadcasted_iota(jnp.int32, (1, 32), 1)
    row_at = lax.broadcasted_iota(jnp.int32, (NZ, 32), 0)
    well_row = lax.broadcasted_iota(jnp.int32, (NW, NY), 0)
    well_col = lax.broadcasted_iota(jnp.int32, (NW, NY), 1)

    def wells(s, carry):
        row_of = jnp.full((1, 32), -1, jnp.int32)
        col_of = jnp.zeros((NW, NY), jnp.int32)
        step_of = jnp.zeros((NW, NY), jnp.int32)
        amounts = [jnp.zeros((NW, NY), f32)] * 3
        for w in range(NW):
            cell = well_cell[s, w]
            row = ((cell - space * (SL * NZ * NY)) >> 8) + NZ
            row_of = jnp.where(lane % NW == w, row, row_of)
            col_of = jnp.where(well_row == w, cell & 255, col_of)
            step_of = jnp.where(well_row == w, sample_step[s, w], step_of)
            amounts = [
                jnp.where(well_row == w, well_misfit[sp, s, w], amounts[sp]) for sp in range(3)
            ]
        row_of = jnp.where(lane < 3 * NW, row_of, -1)
        for x in range(SL + 2):
            hot[s, x] = jnp.where(row_at + x * NZ == row_of, 1.0, 0.0).astype(bf16)
        here = well_col == col_of
        for n in (1, 2):
            chosen = here & (step_of == n)
            for sp in range(3):
                value = jnp.where(chosen, amounts[sp], 0.0)
                high = value.astype(bf16).astype(f32)
                rest = value - high
                middle = rest.astype(bf16).astype(f32)
                low = rest - middle
                inject[n, s, :, sp * NY : (sp + 1) * NY] = jnp.concatenate(
                    [high, middle, low, jnp.zeros((NW, NY), f32)], axis=0
                ).astype(bf16)
        return carry

    lax.fori_loop(0, NSC, wells, 0)

    def x_face(n, adj, s, x, keep=False):
        total = total_x[x]
        for sp in range(3):
            step_a = adj[s, sp, x + 1].astype(f32) - adj[s, sp, x].astype(f32)
            step_c = conc[n, s, sp, x + 1].astype(f32) - conc[n, s, sp, x].astype(f32)
            through = weight_x[sp, x] * step_a
            total = total + step_c * through
            if keep:
                flux[s, sp, x] = through
        total_x[x] = total

    def injected(n, s, x):
        added = mm(hot[s, x], inject[n, s])
        return [added[:, sp * NY : (sp + 1) * NY] for sp in range(3)]

    def layer(n, adj, new, s, x, side=None, face=True):
        own = x - 1
        three = conc[n, s, :, x].reshape(3 * NZ, NY)
        steps_y = mm(three, tabs[4, 0])
        steps_z = mm(tabs[4, 1, 0 : 3 * NZ, 0 : 3 * NZ], three)
        conc_here = [conc[n, s, sp, x].astype(f32) for sp in range(3)]
        adj_here = [adj[s, sp, x].astype(f32) for sp in range(3)]
        sum_z = total_z[own]
        sum_y = total_y[own]
        if face:
            sum_x = total_x[x]
        spread = []
        for sp in range(3):
            a = adj_here[sp]
            rows = slice(sp * NZ, (sp + 1) * NZ)
            flux_z = weight_z[sp, own] * (pltpu.roll(a, NZ - 1, 0) - a)
            flux_y = weight_y[sp, own] * (pltpu.roll(a, NY - 1, 1) - a)
            sum_z = sum_z + steps_z[rows] * flux_z
            sum_y = sum_y + steps_y[rows] * flux_y
            if face:
                flux_x = weight_x[sp, x] * (adj[s, sp, x + 1].astype(f32) - a)
                step_c = conc[n, s, sp, x + 1].astype(f32) - conc_here[sp]
                sum_x = sum_x + step_c * flux_x
                if new is not None:
                    flux[s, sp, x] = flux_x
            elif new is not None:
                flux_x = flux[s, sp, x]
            if new is not None:
                spread.append(
                    (flux_x - flux[s, sp, x - 1])
                    + (flux_z - pltpu.roll(flux_z, 1, 0))
                    + (flux_y - pltpu.roll(flux_y, 1, 1))
                )
        if face:
            total_x[x] = sum_x
        total_z[own] = sum_z
        total_y[own] = sum_y
        donor, acceptor, biomass = conc_here
        donor_inv = 1.0 / (donor_half + donor)
        accept_inv = 1.0 / (acceptor_half + acceptor)
        donor_mono = donor * donor_inv
        accept_mono = acceptor * accept_inv
        both = donor_mono * accept_mono
        stoich = -adj_here[0] - acceptor_yield * adj_here[1] + biomass_yield * adj_here[2]
        scaled = (time_step * stoich) * rate[own]
        growth = scaled * biomass
        total_r[own] = total_r[own] + growth * both
        if new is None:
            return
        spread[0] = spread[0] + (growth * accept_mono) * (donor_half * (donor_inv * donor_inv))
        spread[1] = spread[1] + (growth * donor_mono) * (acceptor_half * (accept_inv * accept_inv))
        spread[2] = spread[2] + scaled * both
        added = injected(n, s, x)
        for sp in range(3):
            if side is not None:
                change[side, s, sp] = spread[sp].astype(bf16)
            new[s, sp, x] = adj_here[sp] + spread[sp] + added[sp]

    def layers(n, adj, new, s, first, last):
        def two(i, carry):
            layer(n, adj, new, s, first + 2 * i)
            layer(n, adj, new, s, first + 2 * i + 1)
            return carry

        lax.fori_loop(0, (last - first) // 2, two, 0)

    def inner(n, adj, new, s):
        x_face(n, adj, s, 1, True)
        layers(n, adj, new, s, 2, SL)

    def outer(n, adj, new, s, sides=(None, None)):
        x_face(n, adj, s, 0, True)
        layer(n, adj, new, s, 1, sides[0], face=False)
        layer(n, adj, new, s, SL, sides[1])

    local[0].wait()
    local[3].wait()
    local[6].wait()

    def inner_two(s, carry):
        inner(2, adj3, adj2, s)
        return carry

    lax.fori_loop(0, NSC, inner_two, 0)
    for copy in cond_halo():
        copy.wait_recv()
    for x, beyond, wall in ((0, 0, space == 0), (SL, SL + 1, space == SP - 1)):
        between = jnp.sqrt(jnp.exp(cond[beyond]) * cond[2 * x + 1 - beyond])
        between = jnp.where(wall, 0.0, between)
        for sp in range(3):
            weight_x[sp, x] = (time_step * diffusion[sp]) * between
    local[4].wait()

    def two_and_one(s, carry):
        for copy in adj_halo(s):
            copy.wait_recv()
        outer(2, adj3, adj2, s, (0, 1))
        for copy in change_halo(s):
            copy.start()
        inner(1, adj2, adj1, s)
        return carry

    lax.fori_loop(0, NSC, two_and_one, 0)
    row = lax.broadcasted_iota(jnp.int32, (NX, LANES), 0)
    col = lax.broadcasted_iota(jnp.int32, (NX, LANES), 1)
    wave_x = jnp.minimum(row, NX - row).astype(f32) * (2.0 * math.pi / NX)
    freq_y = scen * 64 + col % 64
    wave_y = jnp.minimum(freq_y, NY - freq_y).astype(f32) * (2.0 * math.pi / NY)
    freq_z = jnp.full((1, LANES), space, jnp.int32)
    wave_z = jnp.minimum(freq_z, NZ - freq_z).astype(f32) * (2.0 * math.pi / NZ)
    field = (col // 64 + scen) % 2
    length = jnp.where(field == 0, lengths[0], lengths[1])
    square = wave_x * wave_x + wave_z * wave_z + wave_y * wave_y
    spectrum[...] = (length / jnp.sqrt(1.0 + (length * length) * square)) * (1.0 / (NX * NZ * NY))
    local[5].wait()

    def one_and_none(s, carry):
        for copy in change_halo(s):
            copy.wait_recv()
        for side, x in ((0, 0), (1, SL + 1)):
            added = injected(2, s, x)
            for sp in range(3):
                adj2[s, sp, x] = (
                    adj3[s, sp, x].astype(f32) + change_in[side, s, sp].astype(f32) + added[sp]
                )
        for copy in conc_halo(s):
            copy.start()
        outer(1, adj2, adj1, s)
        layers(0, adj1, None, s, 1, SL - 1)
        layer(0, adj1, None, s, SL - 1)
        layer(0, adj1, None, s, SL, face=False)
        return carry

    lax.fori_loop(0, NSC, one_and_none, 0)

    def gradients(x, carry):
        along_z = total_z[x]
        along_y = total_y[x]
        total = along_z + pltpu.roll(along_z, 1, 0) + along_y + pltpu.roll(along_y, 1, 1)
        before = jnp.where(x == 0, 0.0, total_x[x])
        after = jnp.where(x == SL - 1, 0.0, total_x[x + 1])
        grad[0, x] = -0.5 * (total + before + after)
        grad[1, x] = total_r[x]
        return carry

    lax.fori_loop(0, SL, gradients, 0)

    first = lax.broadcasted_iota(jnp.int32, (256, LANES), 1) < 64
    cond_y = times_table(grad[0].reshape(256, NY), tabs[0])
    rate_y = times_table(grad[1].reshape(256, NY), tabs[0])
    for i in range(2):
        lanes = slice(i * LANES, (i + 1) * LANES)
        a = cond_y[:, lanes]
        b = pltpu.roll(rate_y[:, lanes], 64, 1)
        part[0, i] = jnp.where(first, a, b)
        part[1, i] = jnp.where(first, b, a)

    def to_mate(i, source, target):
        return pltpu.make_async_remote_copy(
            src_ref=source,
            dst_ref=target,
            send_sem=sum_send.at[i],
            recv_sem=sum_recv.at[i],
            device_id=(chip * 2 + 1 - core, space),
            device_id_type=MESH,
        )

    part_copy = to_mate(0, part.at[1 - core], part_in)
    part_copy.start()
    part_copy.wait_recv()
    for i in range(2):
        done = table_times(tabs[1], part[core, i] + part_in[i])
        column_out[i, :, 0:SL, :] = done.reshape(SP, SL, LANES)

    def none_faces(s, carry):
        for copy in conc_halo(s):
            copy.wait_recv()
        x_face(0, adj1, s, 0)
        x_face(0, adj1, s, SL)
        return carry

    lax.fori_loop(0, NSC, none_faces, 0)
    faces = jnp.concatenate([total_x[0], total_x[SL]], axis=0) * -0.5
    faces_y = times_table(faces, tabs[0])
    first_rim = lax.broadcasted_iota(jnp.int32, (NZ, LANES), 1) < 64
    for i in range(2):
        lanes = slice(i * LANES, (i + 1) * LANES)
        a = faces_y[0:NZ, lanes]
        b = pltpu.roll(faces_y[NZ : 2 * NZ, lanes], 64, 1)
        rim[0, i] = jnp.where(first_rim, a, b)
        rim[1, i] = jnp.where(first_rim, b, a)
    rim_copy = to_mate(1, rim.at[1 - core], rim_in)
    rim_copy.start()
    rim_copy.wait_recv()
    for i in range(2):
        done = table_times(tabs[3, :, 0:NZ, 0:NZ], rim[core, i] + rim_in[i])
        column_out[i, :, SL : SL + 1, :] = done.reshape(SP, 1, LANES)

    column_copies = []
    for i, (away, offset) in enumerate(offsets_of(2)):
        there = chip if away == 0 else 1 - chip
        other = other_of(offset)
        column_copies.append(
            pltpu.make_async_remote_copy(
                src_ref=column_out.at[there, other],
                dst_ref=column.at[chip, space],
                send_sem=a2a_send.at[i],
                recv_sem=a2a_recv.at[i],
                device_id=(on_chip[away], other),
                device_id_type=MESH,
            )
        )
    for copy in column_copies:
        copy.start()
    column[chip, space] = column_out[chip, space]
    for copy in column_copies:
        copy.wait_recv()
    both = column[0] + column[1]
    field_lanes = lax.broadcasted_iota(jnp.int32, (SP, 1, LANES), 2) // 64 == core
    edge = both[:, SL : SL + 1, :]
    lower = jnp.where(field_lanes, edge, 0.0)
    upper = jnp.where(field_lanes, pltpu.roll(edge.reshape(SP, LANES), 64, 1).reshape(SP, 1, LANES), 0.0)
    at_start = lower + jnp.concatenate([upper[SP - 1 :], upper[: SP - 1]], axis=0)
    at_end = upper + jnp.concatenate([lower[1:], lower[:1]], axis=0)
    place = lax.broadcasted_iota(jnp.int32, (SP, SL, LANES), 1)
    cells = both[:, 0:SL, :]
    cells = cells + jnp.where(place == 0, at_start, 0.0) + jnp.where(place == SL - 1, at_end, 0.0)

    spectral = table_times(tabs[0], cells.reshape(NX, LANES)) * spectrum[...]
    back_out[...] = table_times(tabs[0], spectral).reshape(SP, SL, LANES)

    back_copies = []
    for i, (_, offset) in enumerate(offsets_of(1)):
        other = other_of(offset)
        back_copies.append(
            pltpu.make_async_remote_copy(
                src_ref=back_out.at[other],
                dst_ref=back.at[space],
                send_sem=b2a_send.at[i],
                recv_sem=b2a_recv.at[i],
                device_id=(scen, other),
                device_id_type=MESH,
            )
        )
    for copy in back_copies:
        copy.start()
    back[space] = back_out[space]
    for copy in back_copies:
        copy.wait_recv()

    back_high, back_low = split2(back[...].reshape(256, LANES))
    back_both = jnp.concatenate([back_high, back_low], axis=1)

    def z_blocks(which):
        rows = pl.ds(pl.multiple_of(which * 128, 128), 128)
        high, low = tabs[2, 0, rows, :], tabs[2, 1, rows, :]
        both = mm(high, back_both)
        done = both[:, :LANES] + both[:, LANES:] + mm(low, back_high)
        return done.reshape(2, 64, LANES)

    def block_copy(i, other):
        return pltpu.make_async_remote_copy(
            src_ref=block_out.at[other],
            dst_ref=block.at[scen],
            send_sem=blk_send.at[i],
            recv_sem=blk_recv.at[i],
            device_id=(other, space),
            device_id_type=MESH,
        )

    block_copies = [
        block_copy(1, (1 - chip) * 2 + core),
        block_copy(2, (1 - chip) * 2 + 1 - core),
        block_copy(3, chip * 2 + 1 - core),
    ]
    block_out[pl.ds((1 - chip) * 2, 2)] = z_blocks(1 - chip)
    block_copies[0].start()
    block_copies[1].start()
    block_out[pl.ds(chip * 2, 2)] = z_blocks(chip)
    block_copies[2].start()
    block[scen] = block_out[scen]
    for copy in cond_halo() + (part_copy, rim_copy):
        copy.wait_send()
    for copy in column_copies + back_copies:
        copy.wait_send()
    for s in range(NSC):
        for copy in adj_halo(s) + change_halo(s) + conc_halo(s):
            copy.wait_send()
    for copy in block_copies:
        copy.wait()

    out[...] = block[...]


def along_y(block, tabs, out):
    first = lax.broadcasted_iota(jnp.int32, (64, LANES), 1) < 64
    cond_f = [jnp.where(first, block[i], block[i + 1]) for i in (0, 2)]
    rate_f = [pltpu.roll(jnp.where(first, block[i + 1], block[i]), 64, 1) for i in (0, 2)]
    for which, halves in enumerate((cond_f, rate_f)):
        whole = jnp.concatenate(halves, axis=1)
        out[which] = times_table(whole, tabs).reshape(SL, 8, NY)


def body(states, terminal, log_cond, log_rate, well_cell, sample_step, well_misfit):
    hbm = pl.BlockSpec(memory_space=pltpu.HBM)
    vmem = pl.BlockSpec(memory_space=pltpu.VMEM)
    dma = pltpu.SemaphoreType.DMA
    slab = (SL, NZ, NY)
    scratch = [
        pltpu.VMEM((3, NSC, 3, SL + 2, NZ, NY), bf16),
        pltpu.VMEM((NSC, 3, SL + 2, NZ, NY), bf16),
        pltpu.VMEM((NSC, 3, SL + 2, NZ, NY), f32),
        pltpu.VMEM((NSC, 3, SL + 2, NZ, NY), f32),
        pltpu.VMEM((SL + 2, NZ, NY), f32),
        pltpu.VMEM(slab, f32),
        pltpu.VMEM((3, SL + 1, NZ, NY), f32),
        pltpu.VMEM((3,) + slab, f32),
        pltpu.VMEM((3,) + slab, f32),
        pltpu.VMEM((SL + 1, NZ, NY), f32),
        pltpu.VMEM(slab, f32),
        pltpu.VMEM(slab, f32),
        pltpu.VMEM(slab, f32),
        pltpu.VMEM((2, NSC, 3, NZ, NY), bf16),
        pltpu.VMEM((2, NSC, 3, NZ, NY), bf16),
        pltpu.SMEM((NSC, NW), jnp.int32),
        pltpu.SMEM((NSC, NW), jnp.int32),
        pltpu.SMEM((3, NSC, NW), f32),
        pltpu.VMEM((NSC, SL + 2, NZ, 32), bf16),
        pltpu.VMEM((3, NSC, 32, 3 * NY), bf16),
        pltpu.VMEM((NSC, 3, SL + 1, NZ, NY), f32),
        pltpu.VMEM((5, 2, 256, 256), bf16),
        pltpu.VMEM((NX, LANES), f32),
        pltpu.VMEM((2,) + slab, f32),
        pltpu.VMEM((2, 2, 256, LANES), f32),
        pltpu.VMEM((2, 256, LANES), f32),
        pltpu.VMEM((2, 2, NZ, LANES), f32),
        pltpu.VMEM((2, NZ, LANES), f32),
        pltpu.VMEM((2, SP, SL + 1, LANES), f32),
        pltpu.VMEM((2, SP, SL + 1, LANES), f32),
        pltpu.VMEM((SP, SL, LANES), f32),
        pltpu.VMEM((SP, SL, LANES), f32),
        pltpu.VMEM((4, 64, LANES), f32),
        pltpu.VMEM((4, 64, LANES), f32),
        dma((10,)),
        dma((26,)),
        dma((26,)),
        dma((2,)),
        dma((2,)),
        dma((2 * SP - 1,)),
        dma((2 * SP - 1,)),
        dma((SP - 1,)),
        dma((SP - 1,)),
        dma((4,)),
        dma((4,)),
    ]
    blocks = pl.pallas_call(
        kernel,
        out_shape=jax.ShapeDtypeStruct((4, 64, LANES), f32),
        in_specs=[hbm] * 8,
        out_specs=vmem,
        scratch_shapes=scratch,
        compiler_params=pltpu.CompilerParams(
            collective_id=0, has_side_effects=True, vmem_limit_bytes=40 * 1024 * 1024
        ),
    )(
        *[
            pltpu.with_memory_space_constraint(value, pltpu.HBM)
            for value in (states, terminal, log_cond, log_rate)
        ],
        *[
            pltpu.with_memory_space_constraint(value, pltpu.HBM)
            for value in (well_cell, sample_step, jnp.transpose(well_misfit, (2, 0, 1)))
        ],
        pltpu.with_memory_space_constraint(jnp.asarray(tables()), pltpu.HBM),
    )
    line = jnp.asarray(two_parts(cas(np.arange(256), np.arange(256), 256)))
    return pl.pallas_call(
        along_y,
        out_shape=jax.ShapeDtypeStruct((2, SL, 8, NY), f32),
        in_specs=[vmem, vmem],
        out_specs=vmem,
        compiler_params=pltpu.CompilerParams(vmem_limit_bytes=8 * 1024 * 1024),
    )(blocks, line)


def solution(mesh):
    in_specs = (
        P(None, "scen", None, "space", None, None),
        P("scen", None, "space", None, None),
        P("space", None, None),
        P("space", None, None),
        P("scen", None),
        P("scen", None),
        P("scen", None, None),
    )
    out_specs = P(None, "space", "scen", None)
    return jax.shard_map(body, mesh=mesh, in_specs=in_specs, out_specs=out_specs, check_vma=False)
```

```python
import functools
import math

import jax
import jax.numpy as jnp
import numpy as np
from jax import lax
from jax.experimental import pallas as pl
from jax.experimental.pallas import tpu as pltpu
from jax.sharding import PartitionSpec as P

time_step = 0.05
diffusion = (1.0, 0.8, 0.1)
donor_half = 0.5
acceptor_half = 0.3
acceptor_yield = 0.5
biomass_yield = 0.4
lengths = (40.0, 24.0)
f32 = jnp.float32
bf16 = jnp.bfloat16
MESH = pl.DeviceIdType.MESH

SL = 8
NZ = 32
NY = 256
NSC = 4
NW = 8
SP = 32
NX = SL * SP
LANES = 128


def cas(rows, cols, count):
    angle = 2.0 * np.pi * (np.outer(rows, cols) % count) / count
    return np.cos(angle) + np.sin(angle)


def two_parts(table):
    high = table.astype(np.float32).astype(bf16)
    low = (table - high.astype(np.float64)).astype(np.float32).astype(bf16)
    return np.stack([high, low])


def tables():
    count = np.arange(256)
    line = cas(count, count, 256)
    small = cas(np.arange(NZ), np.arange(NZ), NZ)
    ahead = np.zeros((NZ, SL, SL, NZ))
    back = np.zeros((4, SL, 8, NZ, SL))
    for x in range(SL):
        ahead[:, x, x, :] = small
        back[:, x, :, :, x] = small.reshape(4, 8, NZ)
    corner = np.zeros((256, 256))
    corner[:NZ, :NZ] = small
    turned = [line, ahead.reshape(256, 256), back.reshape(256, 256), corner]
    next_y = np.eye(NY, k=-1) - np.eye(NY)
    next_y[:, -1] = 0.0
    next_z = np.eye(NZ, k=1) - np.eye(NZ)
    next_z[-1] = 0.0
    three = np.zeros((256, 256))
    three[: 3 * NZ, : 3 * NZ] = np.kron(np.eye(3), next_z)
    steps = np.stack([next_y, three]).astype(np.float32).astype(bf16)
    return np.stack([two_parts(table) for table in turned] + [steps])


def offsets_of(chips):
    found = []
    for away in range(chips):
        for i in range(SP):
            x, z, y = i // 8, i // 2 % 4, i % 2
            hops = min(x, 4 - x) + min(z, 4 - z) + (1 if away else 2 * y)
            if hops:
                found.append((-hops, i, away, (x, z, y)))
    return [(away, offset) for _, _, away, offset in sorted(found)]


def split2(value):
    high = value.astype(bf16)
    low = (value - high.astype(f32)).astype(bf16)
    return high, low


def mm(a, b):
    return jnp.dot(a, b, preferred_element_type=f32)


def table_times(table, data):
    high, low = split2(data)
    width = data.shape[1]
    both = mm(table[0], jnp.concatenate([high, low], axis=1))
    return both[:, :width] + both[:, width:] + mm(table[1], high)


def times_table(data, table):
    high, low = split2(data)
    return mm(high, table[0]) + mm(low, table[0]) + mm(high, table[1])


def kernel(
    states,
    terminal,
    log_cond,
    log_rate,
    cell_hbm,
    sample_hbm,
    misfit_hbm,
    tabs_hbm,
    out,
    conc,
    adj3,
    adj2,
    adj1,
    cond,
    rate,
    weight_x,
    weight_z,
    weight_y,
    total_x,
    total_z,
    total_y,
    total_r,
    change,
    change_in,
    well_cell,
    sample_step,
    well_misfit,
    hot,
    inject,
    flux,
    tabs,
    spectrum,
    grad,
    part,
    part_in,
    rim,
    rim_in,
    column_out,
    column,
    back_out,
    back,
    block_out,
    block,
    local_sem,
    halo_send,
    halo_recv,
    sum_send,
    sum_recv,
    a2a_send,
    a2a_recv,
    b2a_send,
    b2a_recv,
    blk_send,
    blk_recv,
):
    scen = lax.axis_index("scen")
    space = lax.axis_index("space")
    chip = scen // 2
    core = lax.rem(scen, 2)
    left = lax.rem(space + SP - 1, SP)
    right = lax.rem(space + 1, SP)

    local = [
        pltpu.make_async_copy(terminal, adj3.at[:, :, 1 : 1 + SL], local_sem.at[0]),
        pltpu.make_async_copy(log_cond, cond.at[1 : 1 + SL], local_sem.at[1]),
        pltpu.make_async_copy(log_rate, rate, local_sem.at[2]),
        pltpu.make_async_copy(states.at[2], conc.at[2, :, :, 1 : 1 + SL], local_sem.at[3]),
        pltpu.make_async_copy(states.at[1], conc.at[1, :, :, 1 : 1 + SL], local_sem.at[4]),
        pltpu.make_async_copy(states.at[0], conc.at[0, :, :, 1 : 1 + SL], local_sem.at[5]),
        pltpu.make_async_copy(tabs_hbm, tabs, local_sem.at[6]),
        pltpu.make_async_copy(cell_hbm, well_cell, local_sem.at[7]),
        pltpu.make_async_copy(sample_hbm, sample_step, local_sem.at[8]),
        pltpu.make_async_copy(misfit_hbm, well_misfit, local_sem.at[9]),
    ]
    for i in (1, 2, 7, 8, 9, 0, 3, 6, 4, 5):
        local[i].start()

    part_x = [lax.rem(space // 8 + i, 4) * 8 for i in range(4)]
    part_z = [lax.rem(space // 2 + i, 4) * 2 for i in range(4)]
    part_y = [lax.rem(space + i, 2) for i in range(2)]
    on_chip = [chip * 2 + core, (1 - chip) * 2 + core]

    def other_of(offset):
        return part_x[offset[0]] + part_z[offset[1]] + part_y[offset[2]]

    barrier = pltpu.get_barrier_semaphore()

    def signal(to_scen, to_space):
        pl.semaphore_signal(
            barrier, inc=1, device_id=(to_scen, to_space), device_id_type=MESH
        )

    for away, offset in offsets_of(2):
        signal(on_chip[away], other_of(offset))
    signal(chip * 2 + 1 - core, space)
    signal((1 - chip) * 2 + 1 - core, space)
    pl.semaphore_wait(barrier, 2 * (SP - 1) + 3)

    def to_side(i, source, target, side):
        return pltpu.make_async_remote_copy(
            src_ref=source,
            dst_ref=target,
            send_sem=halo_send.at[i],
            recv_sem=halo_recv.at[i],
            device_id=(scen, side),
            device_id_type=MESH,
        )

    def cond_halo():
        return (
            to_side(0, log_cond.at[SL - 1], cond.at[0], right),
            to_side(1, log_cond.at[0], cond.at[SL + 1], left),
        )

    def adj_halo(s):
        return (
            to_side(2 + s, terminal.at[s, :, SL - 1], adj3.at[s, :, 0], right),
            to_side(6 + s, terminal.at[s, :, 0], adj3.at[s, :, SL + 1], left),
        )

    def change_halo(s):
        return (
            to_side(10 + s, change.at[1, s], change_in.at[0, s], right),
            to_side(14 + s, change.at[0, s], change_in.at[1, s], left),
        )

    def conc_halo(s):
        return (
            to_side(18 + s, states.at[0, s, :, SL - 1], conc.at[0, s, :, 0], right),
            to_side(22 + s, states.at[0, s, :, 0], conc.at[0, s, :, SL + 1], left),
        )

    for copy in cond_halo():
        copy.start()
    for s in range(NSC):
        for copy in adj_halo(s):
            copy.start()

    nothing = jnp.zeros((NZ, NY), f32)
    for s in range(NSC):
        for sp in range(3):
            for side in (0, SL + 1):
                conc[1, s, sp, side] = nothing.astype(bf16)
                conc[2, s, sp, side] = nothing.astype(bf16)
                adj1[s, sp, side] = nothing

    def clear(x, carry):
        total_x[x] = nothing
        total_z[x] = nothing
        total_y[x] = nothing
        total_r[x] = nothing
        return carry

    lax.fori_loop(0, SL, clear, 0)
    total_x[SL] = nothing

    local[1].wait()
    local[2].wait()
    z_index = lax.broadcasted_iota(jnp.int32, (NZ, NY), 0)
    y_index = lax.broadcasted_iota(jnp.int32, (NZ, NY), 1)

    def own_weights(x, carry):
        here = jnp.exp(cond[x])
        cond[x] = here
        rate[x - 1] = jnp.exp(rate[x - 1])
        above = jnp.sqrt(here * pltpu.roll(here, NZ - 1, 0))
        above = jnp.where(z_index == NZ - 1, 0.0, above)
        beside = jnp.sqrt(here * pltpu.roll(here, NY - 1, 1))
        beside = jnp.where(y_index == NY - 1, 0.0, beside)
        for sp in range(3):
            weight_z[sp, x - 1] = (time_step * diffusion[sp]) * above
            weight_y[sp, x - 1] = (time_step * diffusion[sp]) * beside
        return carry

    lax.fori_loop(1, SL + 1, own_weights, 0)

    def inner_weights(x, carry):
        between = jnp.sqrt(cond[x] * cond[x + 1])
        for sp in range(3):
            weight_x[sp, x] = (time_step * diffusion[sp]) * between
        return carry

    lax.fori_loop(1, SL, inner_weights, 0)

    for i in (7, 8, 9):
        local[i].wait()
    lane = lax.broadcasted_iota(jnp.int32, (1, 32), 1)
    row_at = lax.broadcasted_iota(jnp.int32, (NZ, 32), 0)
    well_row = lax.broadcasted_iota(jnp.int32, (NW, NY), 0)
    well_col = lax.broadcasted_iota(jnp.int32, (NW, NY), 1)

    def wells(s, carry):
        row_of = jnp.full((1, 32), -1, jnp.int32)
        col_of = jnp.zeros((NW, NY), jnp.int32)
        step_of = jnp.zeros((NW, NY), jnp.int32)
        amounts = [jnp.zeros((NW, NY), f32)] * 3
        for w in range(NW):
            cell = well_cell[s, w]
            row = ((cell - space * (SL * NZ * NY)) >> 8) + NZ
            row_of = jnp.where(lane % NW == w, row, row_of)
            col_of = jnp.where(well_row == w, cell & 255, col_of)
            step_of = jnp.where(well_row == w, sample_step[s, w], step_of)
            amounts = [
                jnp.where(well_row == w, well_misfit[sp, s, w], amounts[sp]) for sp in range(3)
            ]
        row_of = jnp.where(lane < 3 * NW, row_of, -1)
        for x in range(SL + 2):
            hot[s, x] = jnp.where(row_at + x * NZ == row_of, 1.0, 0.0).astype(bf16)
        here = well_col == col_of
        for n in (1, 2):
            chosen = here & (step_of == n)
            for sp in range(3):
                value = jnp.where(chosen, amounts[sp], 0.0)
                high = value.astype(bf16).astype(f32)
                rest = value - high
                middle = rest.astype(bf16).astype(f32)
                low = rest - middle
                inject[n, s, :, sp * NY : (sp + 1) * NY] = jnp.concatenate(
                    [high, middle, low, jnp.zeros((NW, NY), f32)], axis=0
                ).astype(bf16)
        return carry

    lax.fori_loop(0, NSC, wells, 0)

    def x_face(n, adj, s, x, keep=False):
        total = total_x[x]
        for sp in range(3):
            step_a = adj[s, sp, x + 1].astype(f32) - adj[s, sp, x].astype(f32)
            step_c = conc[n, s, sp, x + 1].astype(f32) - conc[n, s, sp, x].astype(f32)
            through = weight_x[sp, x] * step_a
            total = total + step_c * through
            if keep:
                flux[s, sp, x] = through
        total_x[x] = total

    def injected(n, s, x):
        added = mm(hot[s, x], inject[n, s])
        return [added[:, sp * NY : (sp + 1) * NY] for sp in range(3)]

    def layer(n, adj, new, s, x, side=None, face=True):
        own = x - 1
        three = conc[n, s, :, x].reshape(3 * NZ, NY)
        steps_y = mm(three, tabs[4, 0])
        steps_z = mm(tabs[4, 1, 0 : 3 * NZ, 0 : 3 * NZ], three)
        conc_here = [conc[n, s, sp, x].astype(f32) for sp in range(3)]
        adj_here = [adj[s, sp, x].astype(f32) for sp in range(3)]
        sum_z = total_z[own]
        sum_y = total_y[own]
        if face:
            sum_x = total_x[x]
        spread = []
        for sp in range(3):
            a = adj_here[sp]
            rows = slice(sp * NZ, (sp + 1) * NZ)
            flux_z = weight_z[sp, own] * (pltpu.roll(a, NZ - 1, 0) - a)
            flux_y = weight_y[sp, own] * (pltpu.roll(a, NY - 1, 1) - a)
            sum_z = sum_z + steps_z[rows] * flux_z
            sum_y = sum_y + steps_y[rows] * flux_y
            if face:
                flux_x = weight_x[sp, x] * (adj[s, sp, x + 1].astype(f32) - a)
                step_c = conc[n, s, sp, x + 1].astype(f32) - conc_here[sp]
                sum_x = sum_x + step_c * flux_x
                if new is not None:
                    flux[s, sp, x] = flux_x
            elif new is not None:
                flux_x = flux[s, sp, x]
            if new is not None:
                spread.append(
                    (flux_x - flux[s, sp, x - 1])
                    + (flux_z - pltpu.roll(flux_z, 1, 0))
                    + (flux_y - pltpu.roll(flux_y, 1, 1))
                )
        if face:
            total_x[x] = sum_x
        total_z[own] = sum_z
        total_y[own] = sum_y
        donor, acceptor, biomass = conc_here
        donor_inv = 1.0 / (donor_half + donor)
        accept_inv = 1.0 / (acceptor_half + acceptor)
        donor_mono = donor * donor_inv
        accept_mono = acceptor * accept_inv
        both = donor_mono * accept_mono
        stoich = -adj_here[0] - acceptor_yield * adj_here[1] + biomass_yield * adj_here[2]
        scaled = (time_step * stoich) * rate[own]
        growth = scaled * biomass
        total_r[own] = total_r[own] + growth * both
        if new is None:
            return
        spread[0] = spread[0] + (growth * accept_mono) * (donor_half * (donor_inv * donor_inv))
        spread[1] = spread[1] + (growth * donor_mono) * (acceptor_half * (accept_inv * accept_inv))
        spread[2] = spread[2] + scaled * both
        added = injected(n, s, x)
        for sp in range(3):
            if side is not None:
                change[side, s, sp] = spread[sp].astype(bf16)
            new[s, sp, x] = adj_here[sp] + spread[sp] + added[sp]

    def layers(n, adj, new, s, first, last):
        def two(i, carry):
            layer(n, adj, new, s, first + 2 * i)
            layer(n, adj, new, s, first + 2 * i + 1)
            return carry

        lax.fori_loop(0, (last - first) // 2, two, 0)

    def inner(n, adj, new, s):
        x_face(n, adj, s, 1, True)
        layers(n, adj, new, s, 2, SL)

    def outer(n, adj, new, s, sides=(None, None)):
        x_face(n, adj, s, 0, True)
        layer(n, adj, new, s, 1, sides[0], face=False)
        layer(n, adj, new, s, SL, sides[1])

    local[0].wait()
    local[3].wait()
    local[6].wait()

    def inner_two(s, carry):
        inner(2, adj3, adj2, s)
        return carry

    lax.fori_loop(0, NSC, inner_two, 0)
    for copy in cond_halo():
        copy.wait_recv()
    for x, beyond, wall in ((0, 0, space == 0), (SL, SL + 1, space == SP - 1)):
        between = jnp.sqrt(jnp.exp(cond[beyond]) * cond[2 * x + 1 - beyond])
        between = jnp.where(wall, 0.0, between)
        for sp in range(3):
            weight_x[sp, x] = (time_step * diffusion[sp]) * between
    local[4].wait()

    def two_and_one(s, carry):
        for copy in adj_halo(s):
            copy.wait_recv()
        outer(2, adj3, adj2, s, (0, 1))
        for copy in change_halo(s):
            copy.start()
        inner(1, adj2, adj1, s)
        return carry

    lax.fori_loop(0, NSC, two_and_one, 0)
    row = lax.broadcasted_iota(jnp.int32, (NX, LANES), 0)
    col = lax.broadcasted_iota(jnp.int32, (NX, LANES), 1)
    wave_x = jnp.minimum(row, NX - row).astype(f32) * (2.0 * math.pi / NX)
    freq_y = scen * 64 + col % 64
    wave_y = jnp.minimum(freq_y, NY - freq_y).astype(f32) * (2.0 * math.pi / NY)
    freq_z = jnp.full((1, LANES), space, jnp.int32)
    wave_z = jnp.minimum(freq_z, NZ - freq_z).astype(f32) * (2.0 * math.pi / NZ)
    field = (col // 64 + scen) % 2
    length = jnp.where(field == 0, lengths[0], lengths[1])
    square = wave_x * wave_x + wave_z * wave_z + wave_y * wave_y
    spectrum[...] = (length / jnp.sqrt(1.0 + (length * length) * square)) * (1.0 / (NX * NZ * NY))
    local[5].wait()

    def one_and_none(s, carry):
        for copy in change_halo(s):
            copy.wait_recv()
        for side, x in ((0, 0), (1, SL + 1)):
            added = injected(2, s, x)
            for sp in range(3):
                adj2[s, sp, x] = (
                    adj3[s, sp, x].astype(f32) + change_in[side, s, sp].astype(f32) + added[sp]
                )
        for copy in conc_halo(s):
            copy.start()
        outer(1, adj2, adj1, s)
        layers(0, adj1, None, s, 1, SL - 1)
        layer(0, adj1, None, s, SL - 1)
        layer(0, adj1, None, s, SL, face=False)
        return carry

    lax.fori_loop(0, NSC, one_and_none, 0)

    def gradients(x, carry):
        along_z = total_z[x]
        along_y = total_y[x]
        total = along_z + pltpu.roll(along_z, 1, 0) + along_y + pltpu.roll(along_y, 1, 1)
        before = jnp.where(x == 0, 0.0, total_x[x])
        after = jnp.where(x == SL - 1, 0.0, total_x[x + 1])
        grad[0, x] = -0.5 * (total + before + after)
        grad[1, x] = total_r[x]
        return carry

    lax.fori_loop(0, SL, gradients, 0)

    first = lax.broadcasted_iota(jnp.int32, (256, LANES), 1) < 64
    cond_y = times_table(grad[0].reshape(256, NY), tabs[0])
    rate_y = times_table(grad[1].reshape(256, NY), tabs[0])
    for i in range(2):
        lanes = slice(i * LANES, (i + 1) * LANES)
        a = cond_y[:, lanes]
        b = pltpu.roll(rate_y[:, lanes], 64, 1)
        part[0, i] = jnp.where(first, a, b)
        part[1, i] = jnp.where(first, b, a)

    def to_mate(i, source, target):
        return pltpu.make_async_remote_copy(
            src_ref=source,
            dst_ref=target,
            send_sem=sum_send.at[i],
            recv_sem=sum_recv.at[i],
            device_id=(chip * 2 + 1 - core, space),
            device_id_type=MESH,
        )

    part_copy = to_mate(0, part.at[1 - core], part_in)
    part_copy.start()
    part_copy.wait_recv()
    for i in range(2):
        done = table_times(tabs[1], part[core, i] + part_in[i])
        column_out[i, :, 0:SL, :] = done.reshape(SP, SL, LANES)

    def none_faces(s, carry):
        for copy in conc_halo(s):
            copy.wait_recv()
        x_face(0, adj1, s, 0)
        x_face(0, adj1, s, SL)
        return carry

    lax.fori_loop(0, NSC, none_faces, 0)
    faces = jnp.concatenate([total_x[0], total_x[SL]], axis=0) * -0.5
    faces_y = times_table(faces, tabs[0])
    first_rim = lax.broadcasted_iota(jnp.int32, (NZ, LANES), 1) < 64
    for i in range(2):
        lanes = slice(i * LANES, (i + 1) * LANES)
        a = faces_y[0:NZ, lanes]
        b = pltpu.roll(faces_y[NZ : 2 * NZ, lanes], 64, 1)
        rim[0, i] = jnp.where(first_rim, a, b)
        rim[1, i] = jnp.where(first_rim, b, a)
    rim_copy = to_mate(1, rim.at[1 - core], rim_in)
    rim_copy.start()
    rim_copy.wait_recv()
    for i in range(2):
        done = table_times(tabs[3, :, 0:NZ, 0:NZ], rim[core, i] + rim_in[i])
        column_out[i, :, SL : SL + 1, :] = done.reshape(SP, 1, LANES)

    column_copies = []
    for i, (away, offset) in enumerate(offsets_of(2)):
        there = chip if away == 0 else 1 - chip
        other = other_of(offset)
        column_copies.append(
            pltpu.make_async_remote_copy(
                src_ref=column_out.at[there, other],
                dst_ref=column.at[chip, space],
                send_sem=a2a_send.at[i],
                recv_sem=a2a_recv.at[i],
                device_id=(on_chip[away], other),
                device_id_type=MESH,
            )
        )
    for copy in column_copies:
        copy.start()
    column[chip, space] = column_out[chip, space]
    for copy in column_copies:
        copy.wait_recv()
    both = column[0] + column[1]
    field_lanes = lax.broadcasted_iota(jnp.int32, (SP, 1, LANES), 2) // 64 == core
    edge = both[:, SL : SL + 1, :]
    lower = jnp.where(field_lanes, edge, 0.0)
    upper = jnp.where(field_lanes, pltpu.roll(edge.reshape(SP, LANES), 64, 1).reshape(SP, 1, LANES), 0.0)
    at_start = lower + jnp.concatenate([upper[SP - 1 :], upper[: SP - 1]], axis=0)
    at_end = upper + jnp.concatenate([lower[1:], lower[:1]], axis=0)
    place = lax.broadcasted_iota(jnp.int32, (SP, SL, LANES), 1)
    cells = both[:, 0:SL, :]
    cells = cells + jnp.where(place == 0, at_start, 0.0) + jnp.where(place == SL - 1, at_end, 0.0)

    spectral = table_times(tabs[0], cells.reshape(NX, LANES)) * spectrum[...]
    back_out[...] = table_times(tabs[0], spectral).reshape(SP, SL, LANES)

    back_copies = []
    for i, (_, offset) in enumerate(offsets_of(1)):
        other = other_of(offset)
        back_copies.append(
            pltpu.make_async_remote_copy(
                src_ref=back_out.at[other],
                dst_ref=back.at[space],
                send_sem=b2a_send.at[i],
                recv_sem=b2a_recv.at[i],
                device_id=(scen, other),
                device_id_type=MESH,
            )
        )
    for copy in back_copies:
        copy.start()
    back[space] = back_out[space]
    for copy in back_copies:
        copy.wait_recv()

    back_high, back_low = split2(back[...].reshape(256, LANES))
    back_both = jnp.concatenate([back_high, back_low], axis=1)

    def z_blocks(which):
        rows = pl.ds(pl.multiple_of(which * 128, 128), 128)
        high, low = tabs[2, 0, rows, :], tabs[2, 1, rows, :]
        both = mm(high, back_both)
        done = both[:, :LANES] + both[:, LANES:] + mm(low, back_high)
        return done.reshape(2, 64, LANES)

    def block_copy(i, other):
        return pltpu.make_async_remote_copy(
            src_ref=block_out.at[other],
            dst_ref=block.at[scen],
            send_sem=blk_send.at[i],
            recv_sem=blk_recv.at[i],
            device_id=(other, space),
            device_id_type=MESH,
        )

    block_copies = [
        block_copy(1, (1 - chip) * 2 + core),
        block_copy(2, (1 - chip) * 2 + 1 - core),
        block_copy(3, chip * 2 + 1 - core),
    ]
    block_out[pl.ds((1 - chip) * 2, 2)] = z_blocks(1 - chip)
    block_copies[0].start()
    block_copies[1].start()
    block_out[pl.ds(chip * 2, 2)] = z_blocks(chip)
    block_copies[2].start()
    block[scen] = block_out[scen]
    for copy in cond_halo() + (part_copy, rim_copy):
        copy.wait_send()
    for copy in column_copies + back_copies:
        copy.wait_send()
    for s in range(NSC):
        for copy in adj_halo(s) + change_halo(s) + conc_halo(s):
            copy.wait_send()
    for copy in block_copies:
        copy.wait()

    out[...] = block[...]


def along_y(block, tabs, out):
    first = lax.broadcasted_iota(jnp.int32, (64, LANES), 1) < 64
    cond_f = [jnp.where(first, block[i], block[i + 1]) for i in (0, 2)]
    rate_f = [pltpu.roll(jnp.where(first, block[i + 1], block[i]), 64, 1) for i in (0, 2)]
    wholes = [jnp.concatenate(halves, axis=1) for halves in (cond_f, rate_f)]
    high, low = split2(jnp.concatenate(wholes, axis=0))
    both = mm(jnp.concatenate([high, low], axis=0), tabs[0])
    done = both[:128] + both[128:] + mm(high, tabs[1])
    out[...] = done.reshape(2, SL, 8, NY)


def body(states, terminal, log_cond, log_rate, well_cell, sample_step, well_misfit):
    hbm = pl.BlockSpec(memory_space=pltpu.HBM)
    vmem = pl.BlockSpec(memory_space=pltpu.VMEM)
    dma = pltpu.SemaphoreType.DMA
    slab = (SL, NZ, NY)
    scratch = [
        pltpu.VMEM((3, NSC, 3, SL + 2, NZ, NY), bf16),
        pltpu.VMEM((NSC, 3, SL + 2, NZ, NY), bf16),
        pltpu.VMEM((NSC, 3, SL + 2, NZ, NY), f32),
        pltpu.VMEM((NSC, 3, SL + 2, NZ, NY), f32),
        pltpu.VMEM((SL + 2, NZ, NY), f32),
        pltpu.VMEM(slab, f32),
        pltpu.VMEM((3, SL + 1, NZ, NY), f32),
        pltpu.VMEM((3,) + slab, f32),
        pltpu.VMEM((3,) + slab, f32),
        pltpu.VMEM((SL + 1, NZ, NY), f32),
        pltpu.VMEM(slab, f32),
        pltpu.VMEM(slab, f32),
        pltpu.VMEM(slab, f32),
        pltpu.VMEM((2, NSC, 3, NZ, NY), bf16),
        pltpu.VMEM((2, NSC, 3, NZ, NY), bf16),
        pltpu.SMEM((NSC, NW), jnp.int32),
        pltpu.SMEM((NSC, NW), jnp.int32),
        pltpu.SMEM((3, NSC, NW), f32),
        pltpu.VMEM((NSC, SL + 2, NZ, 32), bf16),
        pltpu.VMEM((3, NSC, 32, 3 * NY), bf16),
        pltpu.VMEM((NSC, 3, SL + 1, NZ, NY), f32),
        pltpu.VMEM((5, 2, 256, 256), bf16),
        pltpu.VMEM((NX, LANES), f32),
        pltpu.VMEM((2,) + slab, f32),
        pltpu.VMEM((2, 2, 256, LANES), f32),
        pltpu.VMEM((2, 256, LANES), f32),
        pltpu.VMEM((2, 2, NZ, LANES), f32),
        pltpu.VMEM((2, NZ, LANES), f32),
        pltpu.VMEM((2, SP, SL + 1, LANES), f32),
        pltpu.VMEM((2, SP, SL + 1, LANES), f32),
        pltpu.VMEM((SP, SL, LANES), f32),
        pltpu.VMEM((SP, SL, LANES), f32),
        pltpu.VMEM((4, 64, LANES), f32),
        pltpu.VMEM((4, 64, LANES), f32),
        dma((10,)),
        dma((26,)),
        dma((26,)),
        dma((2,)),
        dma((2,)),
        dma((2 * SP - 1,)),
        dma((2 * SP - 1,)),
        dma((SP - 1,)),
        dma((SP - 1,)),
        dma((4,)),
        dma((4,)),
    ]
    blocks = pl.pallas_call(
        kernel,
        out_shape=jax.ShapeDtypeStruct((4, 64, LANES), f32),
        in_specs=[hbm] * 8,
        out_specs=vmem,
        scratch_shapes=scratch,
        compiler_params=pltpu.CompilerParams(
            collective_id=0, has_side_effects=True, vmem_limit_bytes=40 * 1024 * 1024
        ),
    )(
        *[
            pltpu.with_memory_space_constraint(value, pltpu.HBM)
            for value in (states, terminal, log_cond, log_rate)
        ],
        *[
            pltpu.with_memory_space_constraint(value, pltpu.HBM)
            for value in (well_cell, sample_step, jnp.transpose(well_misfit, (2, 0, 1)))
        ],
        pltpu.with_memory_space_constraint(jnp.asarray(tables()), pltpu.HBM),
    )
    line = jnp.asarray(two_parts(cas(np.arange(256), np.arange(256), 256)))
    return pl.pallas_call(
        along_y,
        out_shape=jax.ShapeDtypeStruct((2, SL, 8, NY), f32),
        in_specs=[vmem, vmem],
        out_specs=vmem,
        compiler_params=pltpu.CompilerParams(vmem_limit_bytes=8 * 1024 * 1024),
    )(blocks, line)


def solution(mesh):
    in_specs = (
        P(None, "scen", None, "space", None, None),
        P("scen", None, "space", None, None),
        P("space", None, None),
        P("space", None, None),
        P("scen", None),
        P("scen", None),
        P("scen", None, None),
    )
    out_specs = P(None, "space", "scen", None)
    return jax.shard_map(body, mesh=mesh, in_specs=in_specs, out_specs=out_specs, check_vma=False)
```
